32 devices in a mesh: dp: 8 (over z, core), tensor: 4 (over y, x).
Axes of the slice: x: 2, y: 2, z: 4, core: 2. Of those that a mesh axis runs over, the one named last changes fastest.
Arguments:
- token_ids: int32 [4096], P('dp'), may hold values from 0 to 511
- seq_lengths: int32 [16], P('dp'), may hold values from 32 to 256
- embed_table: bfloat16 [512, 8192], P('dp', 'tensor'), may hold values from -420 to 420
- norm_gain: float32 [8192], replicated, may hold values from 0.1 to 1.9
- query_weight: bfloat16 [8192, 8192], P('tensor', 'dp'), may hold values from -1.3479223 to 1.3479223
- kv_weight: bfloat16 [2048, 8192], P('tensor', 'dp'), may hold values from -0.044194174 to 0.044194174
Outputs:
- attention_out: bfloat16 [4096, 8192], P('dp', 'tensor')
The draws below stay inside these ranges and needn't reach their ends.
All inputs are finite; a program needn't handle non-finite values.
Results may differ from the reference program's by a relative error of at most 0.0091.
Values may be sent and summed in bfloat16 or wider, within the bound.
A program may use at most 128 MiB of HBM per device.

```python
import math
import jax
import jax.numpy as jnp
import numpy as np
from jax import lax

D = 8192
HD = 128
HEADS = 64
KV_HEADS = 8
VOCAB = 512
SEQ = 256
TOKENS = 4096
SEQS = 16


def weights_common(key):
    folded = jax.random.fold_in(key, 101)
    key_keys, key_values, key_noise = jax.random.split(folded, 3)
    key_matrix = jax.random.truncated_normal(key_keys, -4.0, 4.0, (KV_HEADS, HD, D), jnp.float32) * D ** (-0.5)
    value_matrix = jax.random.truncated_normal(key_values, -4.0, 4.0, (KV_HEADS, HD, D), jnp.float32) * D ** (-0.5)
    query_noise = jax.random.truncated_normal(key_noise, -4.0, 4.0, (HEADS, HD, D), jnp.float32) * D ** (-0.5)
    return (key_matrix, value_matrix, query_noise)


def draw_query_weight(key, part):
    key_matrix, value_matrix, query_noise = weights_common(key)
    weights = query_noise
    return weights.reshape(HEADS * HD, D).astype(jnp.bfloat16)


def draw_kv_weight(key, part):
    key_matrix, value_matrix, query_noise = weights_common(key)
    stacked = jnp.stack((key_matrix, value_matrix), axis=0)
    return stacked.reshape(2 * KV_HEADS * HD, D).astype(jnp.bfloat16)


def draw_embed_table(key, part):
    folded = jax.random.fold_in(key, 202)
    key_rows, key_columns, key_entries = jax.random.split(folded, 3)
    column_scale = 3.0 ** (jnp.arange(D, dtype=jnp.float32) / D)[None, :]
    column_scale = column_scale * jnp.exp(jax.random.uniform(key_columns, (1, D), jnp.float32, 0.0, math.log(3.4)))
    row_scale = jnp.exp(jax.random.uniform(key_rows, (VOCAB, 1), jnp.float32, 0.0, math.log(10.0)))
    entries = jax.random.truncated_normal(key_entries, -4.0, 4.0, (VOCAB, D), jnp.float32)
    return (entries * row_scale * column_scale).astype(jnp.bfloat16)


def with_ends(values, own_key, low, top_value):
    extent = values.shape
    spot = [jax.random.randint(jax.random.fold_in(own_key, axis), (), 0, extent[axis]) for axis in range(len(extent))]
    values = values.at[tuple(spot)].set(low)
    longest = extent.index(max(extent))
    spot[longest] = (spot[longest] + 1) % extent[longest]
    return values.at[tuple(spot)].set(top_value)


def rank_table(amount, skew):
    weights = [(1 << 20) // math.isqrt(grade ** skew) + 1 for grade in range(1, amount + 1)]
    scale = 1 + sum(weights) // (1 << 30)
    return np.cumsum(np.array([max(1, weight // scale) for weight in weights]))


def ranked(own_key, shape, amount, lean):
    table = rank_table(amount, lean)
    pick = jax.random.randint(jax.random.fold_in(own_key, 1), shape, 0, int(table[amount - 1]))
    grade = jnp.searchsorted(jnp.asarray(table, jnp.int32), pick, side="right")
    return jax.random.permutation(jax.random.fold_in(own_key, 2), amount)[grade].astype(jnp.int32)


def setup_inputs(seed: int = 0) -> dict:
    key_list = jax.random.split(jax.random.key(seed), 7)
    token_ids = with_ends(ranked(key_list[0], (TOKENS,), VOCAB, 2), jax.random.fold_in(key_list[0], 3), 0, VOCAB - 1).astype(jnp.int32)
    seq_lengths = with_ends(jax.random.randint(key_list[1], (SEQS,), max(1, SEQ // 8), SEQ + 1), jax.random.fold_in(key_list[1], 1), max(1, SEQ // 8), SEQ).astype(jnp.int32)
    embed_table = draw_embed_table(jax.random.fold_in(key_list[6], 71), 0)
    norm_gain = jnp.clip(1.0 + 0.18 * jax.random.normal(key_list[3], (D,), jnp.float32), 0.1, 1.9)
    query_weight = draw_query_weight(jax.random.fold_in(key_list[6], 71), 0)
    kv_weight = draw_kv_weight(jax.random.fold_in(key_list[6], 71), 0)
    return dict(token_ids=token_ids, seq_lengths=seq_lengths, embed_table=embed_table, norm_gain=norm_gain, query_weight=query_weight, kv_weight=kv_weight)


epsilon = 1e-05
rope_base = 500000.0

def rope_tables(positions, head_size):
    halfway = head_size // 2
    frequencies = rope_base ** (-(jnp.arange(halfway, dtype=jnp.float32) * 2.0 / head_size))
    angles = positions.astype(jnp.float32)[:, None] * frequencies[None, :]
    return (jnp.cos(angles), jnp.sin(angles))

def rotate_last(values, cosine, sine_vals):
    halfway = values.shape[-1] // 2
    lower = values[..., :halfway]
    upper = values[..., halfway:]
    return jnp.concatenate([lower * cosine - upper * sine_vals, upper * cosine + lower * sine_vals], axis=-1)

def reference(token_ids, seq_lengths, embed_table, norm_gain, query_weight, kv_weight):
    embedded = embed_table.astype(jnp.float32)[token_ids]
    mean_square = lax.optimization_barrier(jnp.mean(embedded * embedded, axis=1, keepdims=True))
    normed = (embedded * lax.rsqrt(mean_square + epsilon) * norm_gain[None, :]).astype(jnp.bfloat16)
    queries = jnp.dot(normed, query_weight.T, preferred_element_type=jnp.float32)
    keyvals = jnp.dot(normed, kv_weight.T, preferred_element_type=jnp.float32).astype(jnp.bfloat16)
    positions = jnp.arange(TOKENS, dtype=jnp.int32) % SEQ
    cosine, sine_vals = rope_tables(positions, HD)
    cosine = cosine[:, None, :]
    sine_vals = sine_vals[:, None, :]
    rot_queries = rotate_last(queries.reshape(TOKENS, HEADS, HD), cosine, sine_vals).astype(jnp.bfloat16)
    kv_split = keyvals.reshape(TOKENS, 2, KV_HEADS, HD)
    rot_keys = rotate_last(kv_split[:, 0].astype(jnp.float32), cosine, sine_vals).astype(jnp.bfloat16)
    values_all = kv_split[:, 1]
    group_size = HEADS // KV_HEADS

    def attend_one(inputs):
        query_seq, key_seq, value_seq, length = inputs
        key_rep = jnp.repeat(key_seq, group_size, axis=1).astype(jnp.float32)
        value_rep = jnp.repeat(value_seq, group_size, axis=1).astype(jnp.float32)
        scores = jnp.einsum('qhd,khd->hqk', query_seq.astype(jnp.float32), key_rep) / math.sqrt(HD)
        slots = jnp.arange(SEQ, dtype=jnp.int32)
        allowed = (slots[None, :] <= slots[:, None]) & (slots[None, :] < length)
        scores = jnp.where(allowed[None], scores, -1e+30)
        largest = lax.optimization_barrier(jnp.max(scores, axis=-1, keepdims=True))
        exponent = jnp.exp(scores - largest)
        probs = (exponent / lax.optimization_barrier(jnp.sum(exponent, axis=-1, keepdims=True))).astype(jnp.bfloat16)
        attended = jnp.einsum('hqk,khd->qhd', probs.astype(jnp.float32), value_rep)
        return attended.astype(jnp.bfloat16).reshape(SEQ, HEADS * HD)
    per_sequence = lax.map(attend_one, (rot_queries.reshape(SEQS, SEQ, HEADS, HD), rot_keys.reshape(SEQS, SEQ, KV_HEADS, HD), values_all.reshape(SEQS, SEQ, KV_HEADS, HD), seq_lengths))
    return per_sequence.reshape(TOKENS, HEADS * HD)
```

```python
import functools
import math

import jax
import jax.numpy as jnp
import numpy as np
from jax import lax
from jax.experimental import pallas as pl
from jax.experimental.pallas import tpu as pltpu
from jax.sharding import PartitionSpec as P

HD = 128
HEADS = 64
KV_HEADS = 8
SEQ = 256
MESH = pl.DeviceIdType.MESH

epsilon = 1e-05
rope_base = 500000.0


def rope_tables(positions, head_size):
    halfway = head_size // 2
    frequencies = rope_base ** (-(jnp.arange(halfway, dtype=jnp.float32) * 2.0 / head_size))
    angles = positions.astype(jnp.float32)[:, None] * frequencies[None, :]
    return (jnp.cos(angles), jnp.sin(angles))


def rotate_last(values, cosine, sine_vals):
    halfway = values.shape[-1] // 2
    lower = values[..., :halfway]
    upper = values[..., halfway:]
    return jnp.concatenate(
        [lower * cosine - upper * sine_vals, upper * cosine + lower * sine_vals], axis=-1
    )


def general_form(token_ids, seq_lengths, embed_table, norm_gain, query_weight, kv_weight):
    tok_rows = token_ids.shape[0]
    tensor_index = lax.axis_index("tensor")
    heads_here = query_weight.shape[0] // HD
    group_size = HEADS // KV_HEADS
    kv_count = max(1, heads_here // group_size)
    per_group = heads_here // kv_count
    first_kv = tensor_index * heads_here // group_size
    rows = lax.all_gather(embed_table, "tensor", axis=1, tiled=True).astype(jnp.float32)
    mean_square = jnp.mean(rows * rows, axis=1, keepdims=True)
    normed_rows = (rows * lax.rsqrt(mean_square + epsilon) * norm_gain[None, :]).astype(jnp.bfloat16)
    normed = lax.all_to_all(normed_rows, "dp", split_axis=1, concat_axis=0, tiled=True)
    vocab_size = normed.shape[0]
    kv_grid = lax.all_gather(kv_weight, "tensor", axis=0, tiled=True).reshape(2, KV_HEADS, HD, -1)
    kv_rows = lax.dynamic_slice_in_dim(kv_grid, first_kv, kv_count, 1).reshape(2 * kv_count * HD, -1)
    weights = jnp.concatenate([query_weight, kv_rows], axis=0)
    partial = lax.dot_general(
        normed, weights, (((1,), (1,)), ((), ())), preferred_element_type=jnp.float32
    )
    summed = lax.psum_scatter(partial, "dp", scatter_dimension=0, tiled=True)
    table = lax.all_gather(summed.astype(jnp.bfloat16), "dp", axis=0, tiled=True)
    one_hot = (token_ids[:, None] == jnp.arange(vocab_size, dtype=jnp.int32)[None, :]).astype(
        jnp.bfloat16
    )
    picked = jnp.dot(one_hot, table, preferred_element_type=jnp.float32)
    q_width = heads_here * HD
    queries = picked[:, :q_width]
    seq_count = tok_rows // SEQ
    positions = jnp.arange(tok_rows, dtype=jnp.int32) % SEQ
    cosine, sine_vals = rope_tables(positions, HD)
    rot_queries = rotate_last(
        queries.reshape(tok_rows, heads_here, HD), cosine[:, None, :], sine_vals[:, None, :]
    ).astype(jnp.bfloat16)
    local = picked[:, q_width:].reshape(tok_rows, 2, kv_count, HD)
    rot_keys = rotate_last(
        local[:, 0], cosine[:, None, :], sine_vals[:, None, :]
    ).astype(jnp.bfloat16)
    query_grid = rot_queries.reshape(seq_count, SEQ, kv_count, per_group, HD)
    key_grid = rot_keys.reshape(seq_count, SEQ, kv_count, HD)
    value_grid = local[:, 1].astype(jnp.bfloat16).reshape(seq_count, SEQ, kv_count, HD)
    scores = jnp.einsum(
        "sqghd,skgd->sghqk", query_grid, key_grid, preferred_element_type=jnp.float32
    ) / math.sqrt(HD)
    slots = jnp.arange(SEQ, dtype=jnp.int32)
    causal = slots[None, :] <= slots[:, None]
    live = slots[None, :] < seq_lengths[:, None]
    allowed = causal[None, :, :] & live[:, None, :]
    scores = jnp.where(allowed[:, None, None, :, :], scores, -1e30)
    largest = jnp.max(scores, axis=-1, keepdims=True)
    exponent = jnp.exp(scores - largest)
    probs = (exponent / jnp.sum(exponent, axis=-1, keepdims=True)).astype(jnp.bfloat16)
    attended = jnp.einsum(
        "sghqk,skgd->sqghd", probs, value_grid, preferred_element_type=jnp.float32
    )
    return attended.astype(jnp.bfloat16).reshape(tok_rows, heads_here * HD)


NZ = 4
LAG = 3
UNITS = 20
CHUNKS = 2 * UNITS
KD = 1024
VROWS = 512
TOK = 512


def xor2(c, j):
    x, y = lax.rem(c, 2), lax.div(c, 2)
    if j & 1:
        x = 1 - x
    if j & 2:
        y = 1 - y
    return 2 * y + x


def chunk_of(f, j):
    if j == 0:
        return f
    if j == 1:
        return jnp.where(f < 6, 10 + f, 14 + f)
    return jnp.where(f < 2, 16 + 2 * f, 20 + 2 * f) + (j - 2)


def rope_constants():
    freq = rope_base ** (-(np.arange(HD // 2, dtype=np.float64) * 2.0 / HD))
    angle = freq[:, None] * np.arange(SEQ, dtype=np.float64)[None, :]
    scale = math.log2(math.e) / math.sqrt(HD)
    cos, sin = np.cos(angle), np.sin(angle)
    return np.stack([cos * scale, sin * scale, cos, sin]).astype(np.float32)


def fused(
    tok_ref, len_ref, emb_ref, gain_ref, rope_ref, qw_hbm, kvw_hbm, out_hbm,
    w, hop, ein, xin, own, xs, xr, pin, pout, sin, sout, ss_in, ss_own, rinv, tkv, kvt, tq,
    oh, bias, keys, vals, ob,
    w_sem, a_snd, a_rcv, b_snd, b_rcv, e_snd, e_rcv, x_snd, x_rcv, p_snd, p_rcv, s_snd, s_rcv,
    n_snd, n_rcv, kv_snd, kv_rcv, t_snd, t_rcv, o_sem,
):
    f32, bf16 = jnp.float32, jnp.bfloat16
    d = lax.axis_index("dp")
    c = lax.axis_index("tensor")
    z, k = lax.div(d, 2), lax.rem(d, 2)

    def dev(zz, kk, cc):
        return (2 * zz + kk, cc)

    def remote(src, dst, snd, rcv, to):
        return pltpu.make_async_remote_copy(
            src_ref=src, dst_ref=dst, send_sem=snd, recv_sem=rcv, device_id=to, device_id_type=MESH
        )

    barrier = pltpu.get_barrier_semaphore()
    for j in range(4):
        for kk in range(2):
            if j or kk:
                pl.semaphore_signal(
                    barrier, inc=1, device_id=dev(z, lax.rem(k + kk, 2), xor2(c, j)), device_id_type=MESH
                )
    for dz in range(1, NZ):
        for kk in range(2):
            pl.semaphore_signal(
                barrier, inc=1, device_id=dev(lax.rem(z + dz, NZ), kk, c), device_id_type=MESH
            )

    weight_copies = []
    for f in range(10):
        for side in range(2):
            kk = k if side == 0 else 1 - k
            if f < 2:
                src = kvw_hbm.at[pl.ds(pl.multiple_of((2 * kk + f) * 128, 128), 128)]
            else:
                src = qw_hbm.at[pl.ds(pl.multiple_of((f - 2) * 256 + kk * 128, 128), 128)]
            cp = pltpu.make_async_copy(src, w.at[pl.ds(f * 256 + side * 128, 128)], w_sem.at[2 * f + side])
            cp.start()
            weight_copies.append(cp)

    spot = lax.broadcasted_iota(jnp.int32, (128, TOK), 0)
    base = (spot >> 4) * 64 + (spot & 15)
    toks = tok_ref[...]
    for j in range(4):
        hit = (base + 16 * xor2(c, j)) == toks
        oh[pl.ds(128 * j, 128), :] = jnp.where(hit, 1.0, 0.0).astype(bf16)
    kpos = lax.broadcasted_iota(jnp.int32, (SEQ, SEQ), 0)
    qpos = lax.broadcasted_iota(jnp.int32, (SEQ, SEQ), 1)
    for s in range(2):
        good = (kpos <= qpos) & (kpos < len_ref[s])
        bias[s] = jnp.where(good, 0.0, -1e30)
    ss_own[...] = jnp.zeros_like(ss_own)

    @pl.when(z == 0)
    def _():
        pin[...] = jnp.zeros_like(pin)

    @pl.when(z == NZ - 1)
    def _():
        sin[...] = jnp.zeros_like(sin)

    pl.semaphore_wait(barrier, 13)

    def hop_a(j, kk):
        c2, k2 = xor2(c, j), lax.rem(k + kk, 2)
        src = emb_ref.at[pl.ds(pl.multiple_of(16 * c2, 16), 16), pl.ds(pl.multiple_of(KD * k2, KD), KD)]
        dst = hop.at[pl.ds(pl.multiple_of(32 * c + 16 * k, 16), 16)]
        if j or kk:
            return remote(src, dst, a_snd.at[2 * j + kk], a_rcv.at[2 * j + kk], dev(z, k2, c2))
        return pltpu.make_async_copy(src, dst, a_rcv.at[0])

    for j in (3, 1, 2, 0):
        for kk in range(2):
            hop_a(j, kk).start()

    def hop_b(t, src_z):
        src = hop.at[pl.ds(pl.multiple_of(32 * t, 32), 32)]
        dst = ein.at[pl.ds(pl.multiple_of(32 * src_z, 32), 32)]
        return src, dst

    for j in (0, 1, 2, 3):
        for kk in range(2):
            cp = hop_a(j, kk)
            if j or kk:
                cp.wait_recv()
            else:
                cp.wait()
        t = xor2(c, j)
        src, dst = hop_b(t, z)

        @pl.when(t != z)
        def _():
            remote(src, dst, b_snd.at[t], b_rcv.at[z], dev(t, k, c)).start()

        @pl.when(t == z)
        def _():
            pltpu.make_async_copy(src, dst, b_rcv.at[z]).start()

    for t in range(NZ):
        src, dst = hop_b(t, t)
        pltpu.make_async_copy(src, dst, b_rcv.at[t]).wait()

    def hop_c(i):
        frm, half, to, place = (
            (0, 0, 1, 1), (0, 1, 1, 1), (0, 1, 2, 2), (0, 0, 2, 2), (1, 0, 2, 3), (2, 1, 1, 3)
        )[i]
        src = ein.at[pl.ds(128 * frm + 64 * half, 64)]
        dst = ein.at[pl.ds(128 * place + 64 * half, 64)]
        return remote(src, dst, e_snd.at[i], e_rcv.at[i], dev(z, k, xor2(c, to)))

    for i in (0, 2, 1, 3):
        hop_c(i).start()

    gain = gain_ref[:, pl.ds(pl.multiple_of(KD * d, KD), KD)]
    ones = jnp.ones((8, KD), bf16)
    nt = (((1,), (1,)), ((), ()))

    def take(j):
        raw = ein[pl.ds(128 * j, 128), :].astype(f32)
        xin[pl.ds(128 * j, 128), :] = (raw * gain).astype(bf16)
        squares = (raw * raw).astype(bf16)
        ss = lax.dot_general(ones, squares, nt, preferred_element_type=f32)
        ss_own[pl.ds(j, 1), :] = ss[0:1, :]

    take(0)
    for cp in weight_copies:
        cp.wait()

    def x_copy(u):
        return remote(
            xs.at[pl.ds(2 * u, 2)], xr.at[pl.ds(2 * u, 2)], x_snd.at[u], x_rcv.at[u], dev(z, 1 - k, c)
        )

    def unit_wide(u):
        place = jnp.where(u < 5, 0, 1)
        f0 = jnp.where(u < 5, 2 * u, jnp.where(u < 8, 2 * (u - 5), 2 * (u - 7)))
        x = xin[pl.ds(pl.multiple_of(128 * place, 128), 128), :]
        res = lax.dot_general(
            w[pl.ds(pl.multiple_of(256 * f0, 256), 512), :], x, nt, preferred_element_type=f32
        )
        for h in range(2):
            own[2 * u + h] = res[256 * h : 256 * h + 128]
            xs[2 * u + h] = res[256 * h + 128 : 256 * h + 256].astype(bf16)
        x_copy(u).start()

    def unit_deep(u):
        f = jnp.where(u < 10, u - 8, u - 10)
        res = lax.dot_general(
            w[pl.ds(pl.multiple_of(256 * f, 256), 256), :], xin[256:512, :], nt, preferred_element_type=f32
        )
        for h in range(2):
            own[2 * u + h] = res[:128, 128 * h : 128 * h + 128]
            xs[2 * u + h] = res[128:, 128 * h : 128 * h + 128].astype(bf16)
        x_copy(u).start()

    def up_copy(i):
        return remote(pout.at[i], pin.at[i], p_snd.at[i], p_rcv.at[i], dev(lax.rem(z + 1, NZ), k, c))

    def down_copy(i):
        return remote(sout.at[i], sin.at[i], s_snd.at[i], s_rcv.at[i], dev(lax.rem(z + NZ - 1, NZ), k, c))

    def ss_copy(i):
        other = lax.rem(d + i, 2 * NZ)
        return remote(ss_own, ss_in.at[i - 1], n_snd.at[i - 1], n_rcv.at[i - 1], (other, c))

    def t_copy(f):
        return remote(tq.at[f, k], tq.at[f, k], t_snd.at[f], t_rcv.at[f], dev(z, 1 - k, c))

    kv_col = 2 * lax.rem(c, 2) + k
    kv_kind = lax.div(c, 2)

    def kv_copy(f, kk, local):
        dst = kvt.at[kv_kind, f]
        rcv = kv_rcv.at[2 * kv_kind + f]
        if local:
            return pltpu.make_async_copy(tkv.at[f], dst, rcv)
        return remote(tkv.at[f], dst, kv_snd.at[2 * f + kk], rcv, dev(z, kk, kv_col))

    def finish(f, put):
        for j in range(4):
            i = chunk_of(f, j)
            total = own[i] + pin[i].astype(f32) + sin[i].astype(f32)
            put(j, (total * rinv[pl.ds(j, 1), :]).astype(bf16))

    def kv_prepare(g):
        for kind in range(2):
            pltpu.make_async_copy(tkv.at[0], kvt.at[kind, g], kv_rcv.at[2 * kind + g]).wait()
        picked = []
        for kind in range(2):
            acc = jnp.zeros((128, TOK), f32)
            for a in range(4):
                ohg = oh[pl.ds(pl.multiple_of(128 * xor2(c, a), 128), 128), :]
                acc = acc + jnp.dot(kvt[kind, g, a], ohg, preferred_element_type=f32)
            picked.append(acc)
        lo, hi = picked[0][:64], picked[0][64:]
        cos = jnp.concatenate([rope_ref[2]] * 2, axis=1)
        sine = jnp.concatenate([rope_ref[3]] * 2, axis=1)
        rot = jnp.concatenate([lo * cos - hi * sine, hi * cos + lo * sine], axis=0)
        keys[g] = rot.T.astype(bf16)
        vals[g] = picked[1].astype(bf16)

    def out_copy(h):
        return pltpu.make_async_copy(
            ob.at[h], out_hbm.at[:, pl.ds(pl.multiple_of(128 * h, 128), 128)], o_sem.at[h]
        )

    def attend(f, kk):
        g = lax.div(f, 4)
        table = jnp.concatenate([tq[f, kk, j] for j in range(4)], axis=1)
        picked = jnp.dot(table, oh[...], preferred_element_type=f32)
        h = 2 * f + kk
        for s in range(2):
            lo = picked[:64, SEQ * s : SEQ * (s + 1)]
            hi = picked[64:, SEQ * s : SEQ * (s + 1)]
            cos, sine = rope_ref[0], rope_ref[1]
            q = jnp.concatenate([lo * cos - hi * sine, hi * cos + lo * sine], axis=0).astype(bf16)
            sc = jnp.dot(keys[g, pl.ds(SEQ * s, SEQ), :], q, preferred_element_type=f32) + bias[s]
            top = jnp.max(sc, axis=0, keepdims=True)
            e = jnp.exp2(sc - top)
            den = jnp.sum(e, axis=0, keepdims=True)
            o = jnp.dot(vals[g, :, pl.ds(SEQ * s, SEQ)], e.astype(bf16), preferred_element_type=f32)
            ob[h, pl.ds(SEQ * s, SEQ), :] = (o * (1.0 / den)).T.astype(bf16)
        out_copy(h).start()

    unit_wide(jnp.int32(0))

    def step(i, carry):
        even = lax.rem(i, 2) == 0
        u = lax.div(i, 2) + 1

        @pl.when(i == 5)
        def _():
            hop_c(0).wait_recv()
            hop_c(4).start()
            hop_c(2).wait_recv()
            hop_c(5).start()

        @pl.when(i == 8)
        def _():
            hop_c(1).wait_recv()
            take(1)

        @pl.when(i == 14)
        def _():
            hop_c(3).wait_recv()
            take(2)
            hop_c(4).wait_recv()
            hop_c(5).wait_recv()
            take(3)
            for n in range(1, 2 * NZ):
                ss_copy(n).start()

        deep = ((u >= 8) & (u < 10)) | (u >= 12)

        @pl.when(even & (u < UNITS) & deep)
        def _():
            unit_deep(u)

        @pl.when(even & (u < UNITS) & jnp.logical_not(deep))
        def _():
            unit_wide(u)

        @pl.when(even & (u <= UNITS))
        def _():
            x_copy(u - 1).wait_recv()
            for h in range(2):
                own[2 * (u - 1) + h] = own[2 * (u - 1) + h] + xr[2 * (u - 1) + h].astype(f32)

        p = i - LAG * z

        @pl.when((p >= 0) & (p < CHUNKS))
        def _():
            @pl.when(z > 0)
            def _():
                up_copy(p).wait_recv()

            @pl.when(z < NZ - 1)
            def _():
                pout[p] = (own[p] + pin[p].astype(f32)).astype(bf16)
                up_copy(p).start()

        q = i - LAG * (NZ - 1 - z)

        @pl.when((q >= 0) & (q < CHUNKS))
        def _():
            @pl.when(z < NZ - 1)
            def _():
                down_copy(q).wait_recv()

            @pl.when(z > 0)
            def _():
                sout[q] = (own[q] + sin[q].astype(f32)).astype(bf16)
                down_copy(q).start()

        last = i - LAG * (NZ - 1)

        @pl.when(last == 16)
        def _():
            total = ss_own[...]
            for n in range(1, 2 * NZ):
                ss_copy(n).wait_recv()
                total = total + ss_in[n - 1]
            rinv[...] = lax.rsqrt(total * (1.0 / 8192.0) + epsilon)

        @pl.when((last == 17) | (last == 19))
        def _():
            f = lax.div(last - 17, 2)

            def put(j, v):
                tkv[f, xor2(c, j)] = v

            finish(f, put)
            for kk in range(2):
                me = (kv_col == c) & (k == kk)

                @pl.when(me)
                def _():
                    kv_copy(f, kk, True).start()

                @pl.when(jnp.logical_not(me))
                def _():
                    kv_copy(f, kk, False).start()

        @pl.when((last >= 25) & (last < CHUNKS) & (lax.rem(last, 2) == 1))
        def _():
            f = lax.div(last - 25, 2)

            def put(j, v):
                tq[f, k, j] = v

            finish(f + 2, put)
            t_copy(f).start()

        @pl.when(last == 24)
        def _():
            kv_prepare(0)

        @pl.when(last == 27)
        def _():
            kv_prepare(1)

        v = last - 26

        @pl.when(v >= 0)
        def _():
            f = lax.div(v, 2)

            @pl.when(lax.rem(v, 2) == 1)
            def _():
                t_copy(f).wait_recv()

            attend(f, jnp.where(lax.rem(v, 2) == 0, k, 1 - k))

        return carry

    lax.fori_loop(0, CHUNKS + LAG * (NZ - 1) + 2, step, 0)

    for j in range(4):
        for kk in range(2):
            if j or kk:
                hop_a(j, kk).wait_send()
        t = xor2(c, j)

        @pl.when(t != z)
        def _():
            src, dst = hop_b(t, z)
            remote(src, dst, b_snd.at[t], b_rcv.at[z], dev(t, k, c)).wait_send()

    for i in range(6):
        hop_c(i).wait_send()

    def drain_units(u, carry):
        x_copy(u).wait_send()
        return carry

    lax.fori_loop(0, UNITS, drain_units, 0)

    def drain_chunks(i, carry):
        @pl.when(z < NZ - 1)
        def _():
            up_copy(i).wait_send()

        @pl.when(z > 0)
        def _():
            down_copy(i).wait_send()

        return carry

    lax.fori_loop(0, CHUNKS, drain_chunks, 0)
    for n in range(1, 2 * NZ):
        ss_copy(n).wait_send()
    for f in range(2):
        for kk in range(2):

            @pl.when(jnp.logical_not((kv_col == c) & (k == kk)))
            def _():
                kv_copy(f, kk, False).wait_send()

    def drain_heads(f, carry):
        t_copy(f).wait_send()
        out_copy(2 * f).wait()
        out_copy(2 * f + 1).wait()
        return carry

    lax.fori_loop(0, 8, drain_heads, 0)


def square_form(token_ids, seq_lengths, embed_table, norm_gain, query_weight, kv_weight):
    bf16, f32 = jnp.bfloat16, jnp.float32
    vm = pltpu.VMEM
    dma = pltpu.SemaphoreType.DMA
    vspec = pl.BlockSpec(memory_space=pltpu.VMEM)
    aspec = pl.BlockSpec(memory_space=pl.ANY)
    return pl.pallas_call(
        fused,
        out_shape=jax.ShapeDtypeStruct((TOK, 2048), bf16),
        in_specs=[vspec, pl.BlockSpec(memory_space=pltpu.SMEM), vspec, vspec, vspec, aspec, aspec],
        out_specs=aspec,
        scratch_shapes=[
            vm((2560, KD), bf16),
            vm((128, KD), bf16),
            vm((VROWS, KD), bf16),
            vm((VROWS, KD), bf16),
            vm((CHUNKS, 128, 128), f32),
            vm((CHUNKS, 128, 128), bf16),
            vm((CHUNKS, 128, 128), bf16),
            vm((CHUNKS, 128, 128), bf16),
            vm((CHUNKS, 128, 128), bf16),
            vm((CHUNKS, 128, 128), bf16),
            vm((CHUNKS, 128, 128), bf16),
            vm((2 * NZ - 1, 8, 128), f32),
            vm((8, 128), f32),
            vm((8, 128), f32),
            vm((2, 4, 128, 128), bf16),
            vm((2, 2, 4, 128, 128), bf16),
            vm((8, 2, 4, 128, 128), bf16),
            vm((VROWS, TOK), bf16),
            vm((2, SEQ, SEQ), f32),
            vm((2, TOK, 128), bf16),
            vm((2, 128, TOK), bf16),
            vm((16, TOK, 128), bf16),
            dma((20,)),
            dma((8,)), dma((8,)),
            dma((NZ,)), dma((NZ,)),
            dma((6,)), dma((6,)),
            dma((UNITS,)), dma((UNITS,)),
            dma((CHUNKS,)), dma((CHUNKS,)),
            dma((CHUNKS,)), dma((CHUNKS,)),
            dma((2 * NZ - 1,)), dma((2 * NZ - 1,)),
            dma((4,)), dma((4,)),
            dma((8,)), dma((8,)),
            dma((16,)),
        ],
        cost_estimate=pl.CostEstimate(flops=6 * 10**9, bytes_accessed=8 * 10**6, transcendentals=2 * 10**6),
        compiler_params=pltpu.CompilerParams(
            collective_id=0, has_side_effects=True, vmem_limit_bytes=56 * 1024 * 1024
        ),
        name="fused",
    )(
        token_ids.reshape(1, TOK),
        seq_lengths,
        embed_table,
        norm_gain.reshape(1, -1),
        jnp.asarray(rope_constants()),
        query_weight,
        kv_weight,
    )


def solution(mesh):
    dp, tensor = mesh.shape["dp"], mesh.shape["tensor"]
    placed = (P("dp"), P("dp"), P("dp", "tensor"), P(), P("tensor", "dp"), P("tensor", "dp"))

    def on_device(*args):
        tokens, lengths, table, gain, qw, kvw = args
        square = (
            (dp, tensor) == (2 * NZ, 4)
            and tokens.shape == (TOK,)
            and lengths.shape == (2,)
            and table.shape == (64, 2048)
            and qw.shape == (2048, KD)
            and kvw.shape == (512, KD)
        )
        return square_form(*args) if square else general_form(*args)

    return jax.shard_map(
        on_device, mesh=mesh, in_specs=placed, out_specs=P("dp", "tensor"), check_vma=False
    )
```

```python
import functools
import math

import jax
import jax.numpy as jnp
import numpy as np
from jax import lax
from jax.experimental import pallas as pl
from jax.experimental.pallas import tpu as pltpu
from jax.sharding import PartitionSpec as P

HD = 128
HEADS = 64
KV_HEADS = 8
SEQ = 256
MESH = pl.DeviceIdType.MESH

epsilon = 1e-05
rope_base = 500000.0


def rope_tables(positions, head_size):
    halfway = head_size // 2
    frequencies = rope_base ** (-(jnp.arange(halfway, dtype=jnp.float32) * 2.0 / head_size))
    angles = positions.astype(jnp.float32)[:, None] * frequencies[None, :]
    return (jnp.cos(angles), jnp.sin(angles))


def rotate_last(values, cosine, sine_vals):
    halfway = values.shape[-1] // 2
    lower = values[..., :halfway]
    upper = values[..., halfway:]
    return jnp.concatenate(
        [lower * cosine - upper * sine_vals, upper * cosine + lower * sine_vals], axis=-1
    )


def general_form(token_ids, seq_lengths, embed_table, norm_gain, query_weight, kv_weight):
    tok_rows = token_ids.shape[0]
    tensor_index = lax.axis_index("tensor")
    heads_here = query_weight.shape[0] // HD
    group_size = HEADS // KV_HEADS
    kv_count = max(1, heads_here // group_size)
    per_group = heads_here // kv_count
    first_kv = tensor_index * heads_here // group_size
    rows = lax.all_gather(embed_table, "tensor", axis=1, tiled=True).astype(jnp.float32)
    mean_square = jnp.mean(rows * rows, axis=1, keepdims=True)
    normed_rows = (rows * lax.rsqrt(mean_square + epsilon) * norm_gain[None, :]).astype(jnp.bfloat16)
    normed = lax.all_to_all(normed_rows, "dp", split_axis=1, concat_axis=0, tiled=True)
    vocab_size = normed.shape[0]
    kv_grid = lax.all_gather(kv_weight, "tensor", axis=0, tiled=True).reshape(2, KV_HEADS, HD, -1)
    kv_rows = lax.dynamic_slice_in_dim(kv_grid, first_kv, kv_count, 1).reshape(2 * kv_count * HD, -1)
    weights = jnp.concatenate([query_weight, kv_rows], axis=0)
    partial = lax.dot_general(
        normed, weights, (((1,), (1,)), ((), ())), preferred_element_type=jnp.float32
    )
    summed = lax.psum_scatter(partial, "dp", scatter_dimension=0, tiled=True)
    table = lax.all_gather(summed.astype(jnp.bfloat16), "dp", axis=0, tiled=True)
    one_hot = (token_ids[:, None] == jnp.arange(vocab_size, dtype=jnp.int32)[None, :]).astype(
        jnp.bfloat16
    )
    picked = jnp.dot(one_hot, table, preferred_element_type=jnp.float32)
    q_width = heads_here * HD
    queries = picked[:, :q_width]
    seq_count = tok_rows // SEQ
    positions = jnp.arange(tok_rows, dtype=jnp.int32) % SEQ
    cosine, sine_vals = rope_tables(positions, HD)
    rot_queries = rotate_last(
        queries.reshape(tok_rows, heads_here, HD), cosine[:, None, :], sine_vals[:, None, :]
    ).astype(jnp.bfloat16)
    local = picked[:, q_width:].reshape(tok_rows, 2, kv_count, HD)
    rot_keys = rotate_last(
        local[:, 0], cosine[:, None, :], sine_vals[:, None, :]
    ).astype(jnp.bfloat16)
    query_grid = rot_queries.reshape(seq_count, SEQ, kv_count, per_group, HD)
    key_grid = rot_keys.reshape(seq_count, SEQ, kv_count, HD)
    value_grid = local[:, 1].astype(jnp.bfloat16).reshape(seq_count, SEQ, kv_count, HD)
    scores = jnp.einsum(
        "sqghd,skgd->sghqk", query_grid, key_grid, preferred_element_type=jnp.float32
    ) / math.sqrt(HD)
    slots = jnp.arange(SEQ, dtype=jnp.int32)
    causal = slots[None, :] <= slots[:, None]
    live = slots[None, :] < seq_lengths[:, None]
    allowed = causal[None, :, :] & live[:, None, :]
    scores = jnp.where(allowed[:, None, None, :, :], scores, -1e30)
    largest = jnp.max(scores, axis=-1, keepdims=True)
    exponent = jnp.exp(scores - largest)
    probs = (exponent / jnp.sum(exponent, axis=-1, keepdims=True)).astype(jnp.bfloat16)
    attended = jnp.einsum(
        "sghqk,skgd->sqghd", probs, value_grid, preferred_element_type=jnp.float32
    )
    return attended.astype(jnp.bfloat16).reshape(tok_rows, heads_here * HD)


NZ = 4
LAG = 5
UNITS = 20
CHUNKS = 2 * UNITS
KD = 1024
VROWS = 512
TOK = 512


def xor2(c, j):
    x, y = lax.rem(c, 2), lax.div(c, 2)
    if j & 1:
        x = 1 - x
    if j & 2:
        y = 1 - y
    return 2 * y + x


def chunk_of(f, j):
    if j == 0:
        return f
    if j == 1:
        return jnp.where(f < 6, 10 + f, 14 + f)
    return jnp.where(f < 2, 16 + 2 * f, 20 + 2 * f) + (j - 2)


def rope_constants():
    freq = rope_base ** (-(np.arange(HD // 2, dtype=np.float64) * 2.0 / HD))
    angle = freq[:, None] * np.arange(SEQ, dtype=np.float64)[None, :]
    scale = math.log2(math.e) / math.sqrt(HD)
    cos, sin = np.cos(angle), np.sin(angle)
    return np.stack([cos * scale, sin * scale, cos, sin]).astype(np.float32)


def fused(
    tok_ref, len_ref, emb_hbm, gain_hbm, rope_hbm, qw_hbm, kvw_hbm, out_hbm,
    emb_ref, gain_ref, rope,
    w, hop, ein, xin, own, xs, xr, pin, pout, sin, sout, ss_in, ss_own, rinv, tkv, kvt, tq,
    oh, bias, keys, vals, ob,
    i_sem, w_sem, a_snd, a_rcv, b_snd, b_rcv, e_snd, e_rcv, x_snd, x_rcv, p_snd, p_rcv, s_snd, s_rcv,
    n_snd, n_rcv, kv_snd, kv_rcv, t_snd, t_rcv, o_sem,
):
    f32, bf16 = jnp.float32, jnp.bfloat16
    d = lax.axis_index("dp")
    c = lax.axis_index("tensor")
    z, k = lax.div(d, 2), lax.rem(d, 2)

    def dev(zz, kk, cc):
        return (2 * zz + kk, cc)

    def remote(src, dst, snd, rcv, to):
        return pltpu.make_async_remote_copy(
            src_ref=src, dst_ref=dst, send_sem=snd, recv_sem=rcv, device_id=to, device_id_type=MESH
        )

    barrier = pltpu.get_barrier_semaphore()
    for j in range(4):
        for kk in range(2):
            if j or kk:
                pl.semaphore_signal(
                    barrier, inc=1, device_id=dev(z, lax.rem(k + kk, 2), xor2(c, j)), device_id_type=MESH
                )
    for dz in range(1, NZ):
        for kk in range(2):
            pl.semaphore_signal(
                barrier, inc=1, device_id=dev(lax.rem(z + dz, NZ), kk, c), device_id_type=MESH
            )

    emb_copy = pltpu.make_async_copy(emb_hbm, emb_ref, i_sem.at[0])
    emb_copy.start()
    rope_copy = pltpu.make_async_copy(rope_hbm, rope, i_sem.at[1])
    rope_copy.start()
    gain_copy = pltpu.make_async_copy(
        gain_hbm.at[:, pl.ds(pl.multiple_of(KD * d, KD), KD)], gain_ref, i_sem.at[2]
    )
    gain_copy.start()
    weight_copies = []
    for f in range(10):
        for side in range(2):
            kk = k if side == 0 else 1 - k
            if f < 2:
                src = kvw_hbm.at[pl.ds(pl.multiple_of((2 * kk + f) * 128, 128), 128)]
            else:
                src = qw_hbm.at[pl.ds(pl.multiple_of((f - 2) * 256 + kk * 128, 128), 128)]
            cp = pltpu.make_async_copy(src, w.at[pl.ds(f * 256 + side * 128, 128)], w_sem.at[2 * f + side])
            cp.start()
            weight_copies.append(cp)

    spot = lax.broadcasted_iota(jnp.int32, (128, TOK), 0)
    base = (spot >> 4) * 64 + (spot & 15)
    toks = tok_ref[...]
    for j in range(4):
        hit = (base + 16 * xor2(c, j)) == toks
        oh[pl.ds(128 * j, 128), :] = jnp.where(hit, 1.0, 0.0).astype(bf16)
    kpos = lax.broadcasted_iota(jnp.int32, (SEQ, SEQ), 0)
    qpos = lax.broadcasted_iota(jnp.int32, (SEQ, SEQ), 1)
    for s in range(2):
        good = (kpos <= qpos) & (kpos < len_ref[s])
        bias[s] = jnp.where(good, 0.0, -1e30)
    ss_own[...] = jnp.zeros_like(ss_own)

    @pl.when(z == 0)
    def _():
        pin[...] = jnp.zeros_like(pin)

    @pl.when(z == NZ - 1)
    def _():
        sin[...] = jnp.zeros_like(sin)

    emb_copy.wait()
    pl.semaphore_wait(barrier, 13)

    def hop_a(j, kk):
        c2, k2 = xor2(c, j), lax.rem(k + kk, 2)
        src = emb_ref.at[pl.ds(pl.multiple_of(16 * c2, 16), 16), pl.ds(pl.multiple_of(KD * k2, KD), KD)]
        dst = hop.at[pl.ds(pl.multiple_of(32 * c + 16 * k, 16), 16)]
        if j or kk:
            return remote(src, dst, a_snd.at[2 * j + kk], a_rcv.at[2 * j + kk], dev(z, k2, c2))
        return pltpu.make_async_copy(src, dst, a_rcv.at[0])

    for j, kk in ((0, 1), (0, 0), (1, 0), (1, 1), (2, 0), (2, 1), (3, 0), (3, 1)):
        hop_a(j, kk).start()

    def hop_b(t, src_z):
        src = hop.at[pl.ds(pl.multiple_of(32 * t, 32), 32)]
        dst = ein.at[pl.ds(pl.multiple_of(32 * src_z, 32), 32)]
        return src, dst

    for j in (0, 1, 2, 3):
        for kk in range(2):
            cp = hop_a(j, kk)
            if j or kk:
                cp.wait_recv()
            else:
                cp.wait()
        t = xor2(c, j)
        src, dst = hop_b(t, z)

        @pl.when(t != z)
        def _():
            remote(src, dst, b_snd.at[t], b_rcv.at[z], dev(t, k, c)).start()

        @pl.when(t == z)
        def _():
            pltpu.make_async_copy(src, dst, b_rcv.at[z]).start()

    for t in range(NZ):
        src, dst = hop_b(t, t)
        pltpu.make_async_copy(src, dst, b_rcv.at[t]).wait()

    def hop_c(i):
        frm, half, to, place = (
            (0, 0, 1, 1), (0, 1, 1, 1), (0, 1, 2, 2), (0, 0, 2, 2), (1, 0, 2, 3), (2, 1, 1, 3)
        )[i]
        src = ein.at[pl.ds(128 * frm + 64 * half, 64)]
        dst = ein.at[pl.ds(128 * place + 64 * half, 64)]
        return remote(src, dst, e_snd.at[i], e_rcv.at[i], dev(z, k, xor2(c, to)))

    for i in (0, 2, 1, 3):
        hop_c(i).start()

    gain_copy.wait()
    rope_copy.wait()
    gain = gain_ref[...]
    ones = jnp.ones((8, KD), bf16)
    nt = (((1,), (1,)), ((), ()))

    def take(j):
        raw = ein[pl.ds(128 * j, 128), :].astype(f32)
        xin[pl.ds(128 * j, 128), :] = (raw * gain).astype(bf16)
        squares = (raw * raw).astype(bf16)
        ss = lax.dot_general(ones, squares, nt, preferred_element_type=f32)
        ss_own[pl.ds(j, 1), :] = ss[0:1, :]

    take(0)
    for cp in weight_copies:
        cp.wait()

    def x_copy(u):
        return remote(
            xs.at[pl.ds(2 * u, 2)], xr.at[pl.ds(2 * u, 2)], x_snd.at[u], x_rcv.at[u], dev(z, 1 - k, c)
        )

    def unit_wide(u):
        place = jnp.where(u < 5, 0, 1)
        f0 = jnp.where(u < 5, 2 * u, jnp.where(u < 8, 2 * (u - 5), 2 * (u - 7)))
        x = xin[pl.ds(pl.multiple_of(128 * place, 128), 128), :]
        res = lax.dot_general(
            w[pl.ds(pl.multiple_of(256 * f0, 256), 512), :], x, nt, preferred_element_type=f32
        )
        for h in range(2):
            own[2 * u + h] = res[256 * h : 256 * h + 128]
            xs[2 * u + h] = res[256 * h + 128 : 256 * h + 256].astype(bf16)
        x_copy(u).start()

    def unit_deep(u):
        f = jnp.where(u < 10, u - 8, u - 10)
        res = lax.dot_general(
            w[pl.ds(pl.multiple_of(256 * f, 256), 256), :], xin[256:512, :], nt, preferred_element_type=f32
        )
        for h in range(2):
            own[2 * u + h] = res[:128, 128 * h : 128 * h + 128]
            xs[2 * u + h] = res[128:, 128 * h : 128 * h + 128].astype(bf16)
        x_copy(u).start()

    def up_copy(i):
        return remote(pout.at[i], pin.at[i], p_snd.at[i], p_rcv.at[i], dev(lax.rem(z + 1, NZ), k, c))

    def down_copy(i):
        return remote(sout.at[i], sin.at[i], s_snd.at[i], s_rcv.at[i], dev(lax.rem(z + NZ - 1, NZ), k, c))

    def ss_copy(i):
        other = lax.rem(d + i, 2 * NZ)
        return remote(ss_own, ss_in.at[i - 1], n_snd.at[i - 1], n_rcv.at[i - 1], (other, c))

    def t_copy(f):
        return remote(tq.at[f, k], tq.at[f, k], t_snd.at[f], t_rcv.at[f], dev(z, 1 - k, c))

    kv_col = 2 * lax.rem(c, 2) + k
    kv_kind = lax.div(c, 2)

    def kv_copy(f, kk, local):
        dst = kvt.at[kv_kind, f]
        rcv = kv_rcv.at[2 * kv_kind + f]
        if local:
            return pltpu.make_async_copy(tkv.at[f], dst, rcv)
        return remote(tkv.at[f], dst, kv_snd.at[2 * f + kk], rcv, dev(z, kk, kv_col))

    def finish(f, put):
        for j in range(4):
            i = chunk_of(f, j)
            total = own[i] + pin[i].astype(f32) + sin[i].astype(f32)
            put(j, (total * rinv[pl.ds(j, 1), :]).astype(bf16))

    def kv_prepare(g):
        for kind in range(2):
            pltpu.make_async_copy(tkv.at[0], kvt.at[kind, g], kv_rcv.at[2 * kind + g]).wait()
        picked = []
        for kind in range(2):
            acc = jnp.zeros((128, TOK), f32)
            for a in range(4):
                ohg = oh[pl.ds(pl.multiple_of(128 * xor2(c, a), 128), 128), :]
                acc = acc + jnp.dot(kvt[kind, g, a], ohg, preferred_element_type=f32)
            picked.append(acc)
        lo, hi = picked[0][:64], picked[0][64:]
        cos = jnp.concatenate([rope[2]] * 2, axis=1)
        sine = jnp.concatenate([rope[3]] * 2, axis=1)
        rot = jnp.concatenate([lo * cos - hi * sine, hi * cos + lo * sine], axis=0)
        keys[g] = rot.T.astype(bf16)
        vals[g] = picked[1].astype(bf16)

    def out_copy(h):
        return pltpu.make_async_copy(
            ob.at[h], out_hbm.at[:, pl.ds(pl.multiple_of(128 * h, 128), 128)], o_sem.at[h]
        )

    def attend(f):
        g = lax.div(f, 4)
        table = jnp.concatenate(
            [jnp.concatenate([tq[f, kk, j] for j in range(4)], axis=1) for kk in range(2)], axis=0
        )
        picked = jnp.dot(table, oh[...], preferred_element_type=f32)
        cos = jnp.concatenate([rope[0]] * 2, axis=1)
        sine = jnp.concatenate([rope[1]] * 2, axis=1)
        q = []
        for kk in range(2):
            lo, hi = picked[128 * kk : 128 * kk + 64], picked[128 * kk + 64 : 128 * kk + 128]
            q.append(jnp.concatenate([lo * cos - hi * sine, hi * cos + lo * sine], axis=0).astype(bf16))
        blocks = [(s, b) for s in range(2) for b in range(2)]
        scores = []
        for s, b in blocks:
            at = SEQ * s + 128 * b
            both = jnp.concatenate([v[:, at : at + 128] for v in q], axis=1)
            rows = keys[g, pl.ds(SEQ * s, 128 * (b + 1)), :]
            scores.append(jnp.dot(rows, both, preferred_element_type=f32))
        sums = []
        for (s, b), sc in zip(blocks, scores):
            n = 128 * (b + 1)
            es, dens = [], []
            for kk in range(2):
                x = sc[:, 128 * kk : 128 * kk + 128] + bias[s, :n, 128 * b : 128 * b + 128]
                e = jnp.exp2(x - jnp.max(x, axis=0, keepdims=True))
                dens.append(jnp.sum(e, axis=0, keepdims=True))
                es.append(e.astype(bf16))
            o = jnp.dot(
                vals[g, :, pl.ds(SEQ * s, n)], jnp.concatenate(es, axis=1), preferred_element_type=f32
            )
            sums.append((o, dens))
        for (s, b), (o, dens) in zip(blocks, sums):
            for kk in range(2):
                part = o[:, 128 * kk : 128 * kk + 128] * (1.0 / dens[kk])
                ob[2 * f + kk, pl.ds(SEQ * s + 128 * b, 128), :] = part.T.astype(bf16)
        out_copy(2 * f).start()
        out_copy(2 * f + 1).start()

    unit_wide(jnp.int32(0))

    def step(i, carry):
        even = lax.rem(i, 2) == 0
        u = lax.div(i, 2) + 1

        @pl.when(i == 5)
        def _():
            hop_c(0).wait_recv()
            hop_c(4).start()
            hop_c(2).wait_recv()
            hop_c(5).start()

        @pl.when(i == 8)
        def _():
            hop_c(1).wait_recv()
            take(1)

        @pl.when(i == 14)
        def _():
            hop_c(3).wait_recv()
            take(2)
            hop_c(4).wait_recv()
            hop_c(5).wait_recv()
            take(3)
            for n in range(1, 2 * NZ):
                ss_copy(n).start()

        deep = ((u >= 8) & (u < 10)) | (u >= 12)

        @pl.when(even & (u < UNITS) & deep)
        def _():
            unit_deep(u)

        @pl.when(even & (u < UNITS) & jnp.logical_not(deep))
        def _():
            unit_wide(u)

        @pl.when(even & (u <= UNITS))
        def _():
            x_copy(u - 1).wait_recv()
            for h in range(2):
                own[2 * (u - 1) + h] = own[2 * (u - 1) + h] + xr[2 * (u - 1) + h].astype(f32)

        p = i - LAG * z

        @pl.when((p >= 0) & (p < CHUNKS))
        def _():
            @pl.when(z > 0)
            def _():
                up_copy(p).wait_recv()

            @pl.when(z < NZ - 1)
            def _():
                pout[p] = (own[p] + pin[p].astype(f32)).astype(bf16)
                up_copy(p).start()

        q = i - LAG * (NZ - 1 - z)

        @pl.when((q >= 0) & (q < CHUNKS))
        def _():
            @pl.when(z < NZ - 1)
            def _():
                down_copy(q).wait_recv()

            @pl.when(z > 0)
            def _():
                sout[q] = (own[q] + sin[q].astype(f32)).astype(bf16)
                down_copy(q).start()

        last = i - LAG * (NZ - 1)

        @pl.when(last == 16)
        def _():
            total = ss_own[...]
            for n in range(1, 2 * NZ):
                ss_copy(n).wait_recv()
                total = total + ss_in[n - 1]
            rinv[...] = lax.rsqrt(total * (1.0 / 8192.0) + epsilon)

        @pl.when((last == 17) | (last == 19))
        def _():
            f = lax.div(last - 17, 2)

            def put(j, v):
                tkv[f, xor2(c, j)] = v

            finish(f, put)
            for kk in range(2):
                me = (kv_col == c) & (k == kk)

                @pl.when(me)
                def _():
                    kv_copy(f, kk, True).start()

                @pl.when(jnp.logical_not(me))
                def _():
                    kv_copy(f, kk, False).start()

        @pl.when((last >= 25) & (last < CHUNKS) & (lax.rem(last, 2) == 1))
        def _():
            f = lax.div(last - 25, 2)

            def put(j, v):
                tq[f, k, j] = v

            finish(f + 2, put)
            t_copy(f).start()

        @pl.when(last == 24)
        def _():
            kv_prepare(0)

        @pl.when(last == 29)
        def _():
            kv_prepare(1)

        v = last - 28

        @pl.when((v >= 0) & (lax.rem(v, 2) == 0))
        def _():
            t_copy(lax.div(v, 2)).wait_recv()
            attend(lax.div(v, 2))

        return carry

    lax.fori_loop(0, CHUNKS + LAG * (NZ - 1) + 3, step, 0)

    for j in range(4):
        for kk in range(2):
            if j or kk:
                hop_a(j, kk).wait_send()
        t = xor2(c, j)

        @pl.when(t != z)
        def _():
            src, dst = hop_b(t, z)
            remote(src, dst, b_snd.at[t], b_rcv.at[z], dev(t, k, c)).wait_send()

    for i in range(6):
        hop_c(i).wait_send()

    def drain_units(u, carry):
        x_copy(u).wait_send()
        return carry

    lax.fori_loop(0, UNITS, drain_units, 0)

    def drain_chunks(i, carry):
        @pl.when(z < NZ - 1)
        def _():
            up_copy(i).wait_send()

        @pl.when(z > 0)
        def _():
            down_copy(i).wait_send()

        return carry

    lax.fori_loop(0, CHUNKS, drain_chunks, 0)
    for n in range(1, 2 * NZ):
        ss_copy(n).wait_send()
    for f in range(2):
        for kk in range(2):

            @pl.when(jnp.logical_not((kv_col == c) & (k == kk)))
            def _():
                kv_copy(f, kk, False).wait_send()

    def drain_heads(f, carry):
        t_copy(f).wait_send()
        out_copy(2 * f).wait()
        out_copy(2 * f + 1).wait()
        return carry

    lax.fori_loop(0, 8, drain_heads, 0)


def square_form(token_ids, seq_lengths, embed_table, norm_gain, query_weight, kv_weight):
    bf16, f32 = jnp.bfloat16, jnp.float32
    vm = pltpu.VMEM
    dma = pltpu.SemaphoreType.DMA
    vspec = pl.BlockSpec(memory_space=pltpu.VMEM)
    aspec = pl.BlockSpec(memory_space=pl.ANY)
    return pl.pallas_call(
        fused,
        out_shape=jax.ShapeDtypeStruct((TOK, 2048), bf16),
        in_specs=[vspec, pl.BlockSpec(memory_space=pltpu.SMEM), aspec, aspec, aspec, aspec, aspec],
        out_specs=aspec,
        scratch_shapes=[
            vm((64, 2048), bf16),
            vm((1, KD), f32),
            vm((4, HD // 2, SEQ), f32),
            vm((2560, KD), bf16),
            vm((128, KD), bf16),
            vm((VROWS, KD), bf16),
            vm((VROWS, KD), bf16),
            vm((CHUNKS, 128, 128), f32),
            vm((CHUNKS, 128, 128), bf16),
            vm((CHUNKS, 128, 128), bf16),
            vm((CHUNKS, 128, 128), bf16),
            vm((CHUNKS, 128, 128), bf16),
            vm((CHUNKS, 128, 128), bf16),
            vm((CHUNKS, 128, 128), bf16),
            vm((2 * NZ - 1, 8, 128), f32),
            vm((8, 128), f32),
            vm((8, 128), f32),
            vm((2, 4, 128, 128), bf16),
            vm((2, 2, 4, 128, 128), bf16),
            vm((8, 2, 4, 128, 128), bf16),
            vm((VROWS, TOK), bf16),
            vm((2, SEQ, SEQ), f32),
            vm((2, TOK, 128), bf16),
            vm((2, 128, TOK), bf16),
            vm((16, TOK, 128), bf16),
            dma((3,)),
            dma((20,)),
            dma((8,)), dma((8,)),
            dma((NZ,)), dma((NZ,)),
            dma((6,)), dma((6,)),
            dma((UNITS,)), dma((UNITS,)),
            dma((CHUNKS,)), dma((CHUNKS,)),
            dma((CHUNKS,)), dma((CHUNKS,)),
            dma((2 * NZ - 1,)), dma((2 * NZ - 1,)),
            dma((4,)), dma((4,)),
            dma((8,)), dma((8,)),
            dma((16,)),
        ],
        cost_estimate=pl.CostEstimate(flops=6 * 10**9, bytes_accessed=8 * 10**6, transcendentals=2 * 10**6),
        compiler_params=pltpu.CompilerParams(
            collective_id=0, has_side_effects=True, vmem_limit_bytes=56 * 1024 * 1024
        ),
        name="fused",
    )(
        token_ids.reshape(1, TOK),
        seq_lengths,
        embed_table,
        norm_gain.reshape(1, -1),
        jnp.asarray(rope_constants()),
        query_weight,
        kv_weight,
    )


def solution(mesh):
    dp, tensor = mesh.shape["dp"], mesh.shape["tensor"]
    placed = (P("dp"), P("dp"), P("dp", "tensor"), P(), P("tensor", "dp"), P("tensor", "dp"))

    def on_device(*args):
        tokens, lengths, table, gain, qw, kvw = args
        square = (
            (dp, tensor) == (2 * NZ, 4)
            and tokens.shape == (TOK,)
            and lengths.shape == (2,)
            and table.shape == (64, 2048)
            and qw.shape == (2048, KD)
            and kvw.shape == (512, KD)
        )
        return square_form(*args) if square else general_form(*args)

    return jax.shard_map(
        on_device, mesh=mesh, in_specs=placed, out_specs=P("dp", "tensor"), check_vma=False
    )
```

```python
import functools
import math

import jax
import jax.numpy as jnp
import numpy as np
from jax import lax
from jax.experimental import pallas as pl
from jax.experimental.pallas import tpu as pltpu
from jax.sharding import PartitionSpec as P

HD = 128
HEADS = 64
KV_HEADS = 8
SEQ = 256
MESH = pl.DeviceIdType.MESH

epsilon = 1e-05
rope_base = 500000.0


def rope_tables(positions, head_size):
    halfway = head_size // 2
    frequencies = rope_base ** (-(jnp.arange(halfway, dtype=jnp.float32) * 2.0 / head_size))
    angles = positions.astype(jnp.float32)[:, None] * frequencies[None, :]
    return (jnp.cos(angles), jnp.sin(angles))


def rotate_last(values, cosine, sine_vals):
    halfway = values.shape[-1] // 2
    lower = values[..., :halfway]
    upper = values[..., halfway:]
    return jnp.concatenate(
        [lower * cosine - upper * sine_vals, upper * cosine + lower * sine_vals], axis=-1
    )


def general_form(token_ids, seq_lengths, embed_table, norm_gain, query_weight, kv_weight):
    tok_rows = token_ids.shape[0]
    tensor_index = lax.axis_index("tensor")
    heads_here = query_weight.shape[0] // HD
    group_size = HEADS // KV_HEADS
    kv_count = max(1, heads_here // group_size)
    per_group = heads_here // kv_count
    first_kv = tensor_index * heads_here // group_size
    rows = lax.all_gather(embed_table, "tensor", axis=1, tiled=True).astype(jnp.float32)
    mean_square = jnp.mean(rows * rows, axis=1, keepdims=True)
    normed_rows = (rows * lax.rsqrt(mean_square + epsilon) * norm_gain[None, :]).astype(jnp.bfloat16)
    normed = lax.all_to_all(normed_rows, "dp", split_axis=1, concat_axis=0, tiled=True)
    vocab_size = normed.shape[0]
    kv_grid = lax.all_gather(kv_weight, "tensor", axis=0, tiled=True).reshape(2, KV_HEADS, HD, -1)
    kv_rows = lax.dynamic_slice_in_dim(kv_grid, first_kv, kv_count, 1).reshape(2 * kv_count * HD, -1)
    weights = jnp.concatenate([query_weight, kv_rows], axis=0)
    partial = lax.dot_general(
        normed, weights, (((1,), (1,)), ((), ())), preferred_element_type=jnp.float32
    )
    summed = lax.psum_scatter(partial, "dp", scatter_dimension=0, tiled=True)
    table = lax.all_gather(summed.astype(jnp.bfloat16), "dp", axis=0, tiled=True)
    one_hot = (token_ids[:, None] == jnp.arange(vocab_size, dtype=jnp.int32)[None, :]).astype(
        jnp.bfloat16
    )
    picked = jnp.dot(one_hot, table, preferred_element_type=jnp.float32)
    q_width = heads_here * HD
    queries = picked[:, :q_width]
    seq_count = tok_rows // SEQ
    positions = jnp.arange(tok_rows, dtype=jnp.int32) % SEQ
    cosine, sine_vals = rope_tables(positions, HD)
    rot_queries = rotate_last(
        queries.reshape(tok_rows, heads_here, HD), cosine[:, None, :], sine_vals[:, None, :]
    ).astype(jnp.bfloat16)
    local = picked[:, q_width:].reshape(tok_rows, 2, kv_count, HD)
    rot_keys = rotate_last(
        local[:, 0], cosine[:, None, :], sine_vals[:, None, :]
    ).astype(jnp.bfloat16)
    query_grid = rot_queries.reshape(seq_count, SEQ, kv_count, per_group, HD)
    key_grid = rot_keys.reshape(seq_count, SEQ, kv_count, HD)
    value_grid = local[:, 1].astype(jnp.bfloat16).reshape(seq_count, SEQ, kv_count, HD)
    scores = jnp.einsum(
        "sqghd,skgd->sghqk", query_grid, key_grid, preferred_element_type=jnp.float32
    ) / math.sqrt(HD)
    slots = jnp.arange(SEQ, dtype=jnp.int32)
    causal = slots[None, :] <= slots[:, None]
    live = slots[None, :] < seq_lengths[:, None]
    allowed = causal[None, :, :] & live[:, None, :]
    scores = jnp.where(allowed[:, None, None, :, :], scores, -1e30)
    largest = jnp.max(scores, axis=-1, keepdims=True)
    exponent = jnp.exp(scores - largest)
    probs = (exponent / jnp.sum(exponent, axis=-1, keepdims=True)).astype(jnp.bfloat16)
    attended = jnp.einsum(
        "sghqk,skgd->sqghd", probs, value_grid, preferred_element_type=jnp.float32
    )
    return attended.astype(jnp.bfloat16).reshape(tok_rows, heads_here * HD)


NZ = 4
LAG = 5
UNITS = 20
CHUNKS = 2 * UNITS
KD = 1024
VROWS = 512
TOK = 512


def xor2(c, j):
    x, y = lax.rem(c, 2), lax.div(c, 2)
    if j & 1:
        x = 1 - x
    if j & 2:
        y = 1 - y
    return 2 * y + x


def chunk_of(f, j):
    if j == 0:
        return f
    if j == 1:
        return jnp.where(f < 6, 10 + f, 14 + f)
    return jnp.where(f < 2, 16 + 2 * f, 20 + 2 * f) + (j - 2)


def rope_constants():
    freq = rope_base ** (-(np.arange(HD // 2, dtype=np.float64) * 2.0 / HD))
    angle = freq[:, None] * np.arange(SEQ, dtype=np.float64)[None, :]
    scale = math.log2(math.e) / math.sqrt(HD)
    cos, sin = np.cos(angle), np.sin(angle)
    return np.stack([cos * scale, sin * scale, cos, sin]).astype(np.float32)


def fused(
    tok_ref, len_ref, emb_hbm, gain_hbm, rope_hbm, qw_hbm, kvw_hbm, out_ref,
    emb_ref, gain_ref, rope,
    w, hop, ein, xin, own, xs, xr, pin, pout, sin, sout, ss_in, ss_own, rinv, tkv, kvt, tq,
    oh, bias, keys, vals,
    i_sem, w_sem, a_snd, a_rcv, b_snd, b_rcv, e_snd, e_rcv, x_snd, x_rcv, p_snd, p_rcv, s_snd, s_rcv,
    n_snd, n_rcv, kv_snd, kv_rcv, t_snd, t_rcv,
):
    f32, bf16 = jnp.float32, jnp.bfloat16
    d = lax.axis_index("dp")
    c = lax.axis_index("tensor")
    z, k = lax.div(d, 2), lax.rem(d, 2)

    def dev(zz, kk, cc):
        return (2 * zz + kk, cc)

    def remote(src, dst, snd, rcv, to):
        return pltpu.make_async_remote_copy(
            src_ref=src, dst_ref=dst, send_sem=snd, recv_sem=rcv, device_id=to, device_id_type=MESH
        )

    barrier = pltpu.get_barrier_semaphore()
    for j in range(4):
        for kk in range(2):
            if j or kk:
                pl.semaphore_signal(
                    barrier, inc=1, device_id=dev(z, lax.rem(k + kk, 2), xor2(c, j)), device_id_type=MESH
                )
    for dz in range(1, NZ):
        for kk in range(2):
            pl.semaphore_signal(
                barrier, inc=1, device_id=dev(lax.rem(z + dz, NZ), kk, c), device_id_type=MESH
            )

    emb_copy = pltpu.make_async_copy(emb_hbm, emb_ref, i_sem.at[0])
    emb_copy.start()

    emb_copy.wait()
    pl.semaphore_wait(barrier, 13)

    def hop_a(j, kk):
        c2, k2 = xor2(c, j), lax.rem(k + kk, 2)
        src = emb_ref.at[pl.ds(pl.multiple_of(16 * c2, 16), 16), pl.ds(pl.multiple_of(KD * k2, KD), KD)]
        dst = hop.at[pl.ds(pl.multiple_of(32 * c + 16 * k, 16), 16)]
        if j or kk:
            return remote(src, dst, a_snd.at[2 * j + kk], a_rcv.at[2 * j + kk], dev(z, k2, c2))
        return pltpu.make_async_copy(src, dst, a_rcv.at[0])

    for j, kk in ((0, 1), (0, 0), (1, 0), (1, 1), (2, 0), (2, 1), (3, 0), (3, 1)):
        hop_a(j, kk).start()

    rope_copy = pltpu.make_async_copy(rope_hbm, rope, i_sem.at[1])
    rope_copy.start()
    gain_copy = pltpu.make_async_copy(
        gain_hbm.at[:, pl.ds(pl.multiple_of(KD * d, KD), KD)], gain_ref, i_sem.at[2]
    )
    gain_copy.start()
    weight_copies = []
    for f in range(10):
        for side in range(2):
            kk = k if side == 0 else 1 - k
            if f < 2:
                src = kvw_hbm.at[pl.ds(pl.multiple_of((2 * kk + f) * 128, 128), 128)]
            else:
                src = qw_hbm.at[pl.ds(pl.multiple_of((f - 2) * 256 + kk * 128, 128), 128)]
            cp = pltpu.make_async_copy(src, w.at[pl.ds(f * 256 + side * 128, 128)], w_sem.at[2 * f + side])
            cp.start()
            weight_copies.append(cp)

    def hop_b(t, src_z):
        src = hop.at[pl.ds(pl.multiple_of(32 * t, 32), 32)]
        dst = ein.at[pl.ds(pl.multiple_of(32 * src_z, 32), 32)]
        return src, dst

    def pass_on(j):
        for kk in range(2):
            cp = hop_a(j, kk)
            if j or kk:
                cp.wait_recv()
            else:
                cp.wait()
        t = xor2(c, j)
        src, dst = hop_b(t, z)

        @pl.when(t != z)
        def _():
            remote(src, dst, b_snd.at[t], b_rcv.at[z], dev(t, k, c)).start()

        @pl.when(t == z)
        def _():
            pltpu.make_async_copy(src, dst, b_rcv.at[z]).start()

    pass_on(0)
    spot = lax.broadcasted_iota(jnp.int32, (128, TOK), 0)
    base = (spot >> 4) * 64 + (spot & 15)
    toks = tok_ref[...]
    for j in range(4):
        hit = (base + 16 * xor2(c, j)) == toks
        oh[pl.ds(128 * j, 128), :] = jnp.where(hit, 1.0, 0.0).astype(bf16)
    pass_on(1)
    pass_on(2)
    pass_on(3)
    kpos = lax.broadcasted_iota(jnp.int32, (SEQ, SEQ), 0)
    qpos = lax.broadcasted_iota(jnp.int32, (SEQ, SEQ), 1)
    for s in range(2):
        good = (kpos <= qpos) & (kpos < len_ref[s])
        bias[s] = jnp.where(good, 0.0, -1e30)
    ss_own[...] = jnp.zeros_like(ss_own)

    @pl.when(z == 0)
    def _():
        pin[...] = jnp.zeros_like(pin)

    @pl.when(z == NZ - 1)
    def _():
        sin[...] = jnp.zeros_like(sin)

    def piece(n):
        return pl.multiple_of(32 * lax.rem(z + n, NZ), 32)

    def hop_c(place, to, n):
        src = ein.at[pl.ds(128 * place + piece(n), 32)]
        dst = ein.at[pl.ds(128 * (place + to) + piece(n), 32)]
        i = 4 * (place + to - 1) + n
        return remote(src, dst, e_snd.at[i], e_rcv.at[i], dev(z, k, xor2(c, to)))

    for n in (0, 1, 3, 2):
        src, dst = hop_b(lax.rem(z + n, NZ), lax.rem(z + n, NZ))
        pltpu.make_async_copy(src, dst, b_rcv.at[lax.rem(z + n, NZ)]).wait()
        hop_c(0, 1, n).start()
        hop_c(0, 2, n).start()

    gain_copy.wait()
    rope_copy.wait()
    gain = gain_ref[...]
    ones = jnp.ones((8, KD), bf16)
    nt = (((1,), (1,)), ((), ()))

    def take(j):
        raw = ein[pl.ds(128 * j, 128), :].astype(f32)
        xin[pl.ds(128 * j, 128), :] = (raw * gain).astype(bf16)
        squares = (raw * raw).astype(bf16)
        ss = lax.dot_general(ones, squares, nt, preferred_element_type=f32)
        ss_own[pl.ds(j, 1), :] = ss[0:1, :]

    take(0)
    for cp in weight_copies:
        cp.wait()

    def x_copy(u):
        return remote(
            xs.at[pl.ds(2 * u, 2)], xr.at[pl.ds(2 * u, 2)], x_snd.at[u], x_rcv.at[u], dev(z, 1 - k, c)
        )

    def unit_wide(u):
        place = jnp.where(u < 5, 0, 1)
        f0 = jnp.where(u < 5, 2 * u, jnp.where(u < 8, 2 * (u - 5), 2 * (u - 7)))
        x = xin[pl.ds(pl.multiple_of(128 * place, 128), 128), :]
        res = lax.dot_general(
            w[pl.ds(pl.multiple_of(256 * f0, 256), 512), :], x, nt, preferred_element_type=f32
        )
        for h in range(2):
            own[2 * u + h] = res[256 * h : 256 * h + 128]
            xs[2 * u + h] = res[256 * h + 128 : 256 * h + 256].astype(bf16)
        x_copy(u).start()

    def unit_deep(u):
        f = jnp.where(u < 10, u - 8, u - 10)
        res = lax.dot_general(
            w[pl.ds(pl.multiple_of(256 * f, 256), 256), :], xin[256:512, :], nt, preferred_element_type=f32
        )
        for h in range(2):
            own[2 * u + h] = res[:128, 128 * h : 128 * h + 128]
            xs[2 * u + h] = res[128:, 128 * h : 128 * h + 128].astype(bf16)
        x_copy(u).start()

    def up_copy(i):
        return remote(pout.at[i], pin.at[i], p_snd.at[i], p_rcv.at[i], dev(lax.rem(z + 1, NZ), k, c))

    def down_copy(i):
        return remote(sout.at[i], sin.at[i], s_snd.at[i], s_rcv.at[i], dev(lax.rem(z + NZ - 1, NZ), k, c))

    def ss_copy(i):
        other = lax.rem(d + i, 2 * NZ)
        return remote(ss_own, ss_in.at[i - 1], n_snd.at[i - 1], n_rcv.at[i - 1], (other, c))

    def t_copy(f):
        return remote(tq.at[f, k], tq.at[f, k], t_snd.at[f], t_rcv.at[f], dev(z, 1 - k, c))

    kv_col = 2 * lax.rem(c, 2) + k
    kv_kind = lax.div(c, 2)

    def kv_copy(f, kk, local):
        dst = kvt.at[kv_kind, f]
        rcv = kv_rcv.at[2 * kv_kind + f]
        if local:
            return pltpu.make_async_copy(tkv.at[f], dst, rcv)
        return remote(tkv.at[f], dst, kv_snd.at[2 * f + kk], rcv, dev(z, kk, kv_col))

    def finish(f, put):
        for j in range(4):
            i = chunk_of(f, j)
            total = own[i] + pin[i].astype(f32) + sin[i].astype(f32)
            put(j, (total * rinv[pl.ds(j, 1), :]).astype(bf16))

    def kv_prepare(g):
        for kind in range(2):
            pltpu.make_async_copy(tkv.at[0], kvt.at[kind, g], kv_rcv.at[2 * kind + g]).wait()
        picked = []
        for kind in range(2):
            acc = jnp.zeros((128, TOK), f32)
            for a in range(4):
                ohg = oh[pl.ds(pl.multiple_of(128 * xor2(c, a), 128), 128), :]
                acc = acc + jnp.dot(kvt[kind, g, a], ohg, preferred_element_type=f32)
            picked.append(acc)
        lo, hi = picked[0][:64], picked[0][64:]
        cos = jnp.concatenate([rope[2]] * 2, axis=1)
        sine = jnp.concatenate([rope[3]] * 2, axis=1)
        rot = jnp.concatenate([lo * cos - hi * sine, hi * cos + lo * sine], axis=0)
        keys[g] = rot.T.astype(bf16)
        vals[g] = picked[1].astype(bf16)

    def attend(f):
        g = lax.div(f, 4)
        table = jnp.concatenate(
            [jnp.concatenate([tq[f, kk, j] for j in range(4)], axis=1) for kk in range(2)], axis=0
        )
        picked = jnp.dot(table, oh[...], preferred_element_type=f32)
        cos = jnp.concatenate([rope[0]] * 2, axis=1)
        sine = jnp.concatenate([rope[1]] * 2, axis=1)
        q = []
        for kk in range(2):
            lo, hi = picked[128 * kk : 128 * kk + 64], picked[128 * kk + 64 : 128 * kk + 128]
            q.append(jnp.concatenate([lo * cos - hi * sine, hi * cos + lo * sine], axis=0).astype(bf16))
        blocks = [(s, b) for s in range(2) for b in range(2)]
        scores = []
        for s, b in blocks:
            at = SEQ * s + 128 * b
            both = jnp.concatenate([v[:, at : at + 128] for v in q], axis=1)
            rows = keys[g, pl.ds(SEQ * s, 128 * (b + 1)), :]
            scores.append(jnp.dot(rows, both, preferred_element_type=f32))
        sums = []
        for (s, b), sc in zip(blocks, scores):
            n = 128 * (b + 1)
            es, dens = [], []
            for kk in range(2):
                x = sc[:, 128 * kk : 128 * kk + 128] + bias[s, :n, 128 * b : 128 * b + 128]
                e = jnp.exp2(x - jnp.max(x, axis=0, keepdims=True))
                dens.append(jnp.sum(e, axis=0, keepdims=True))
                es.append(e.astype(bf16))
            o = jnp.dot(
                vals[g, :, pl.ds(SEQ * s, n)], jnp.concatenate(es, axis=1), preferred_element_type=f32
            )
            sums.append((o, dens))
        for (s, b), (o, dens) in zip(blocks, sums):
            for kk in range(2):
                part = o[:, 128 * kk : 128 * kk + 128] * (1.0 / dens[kk])
                at = pl.multiple_of(256 * f + 128 * kk, 128)
                out_ref[pl.ds(SEQ * s + 128 * b, 128), pl.ds(at, 128)] = part.T.astype(bf16)

    unit_wide(jnp.int32(0))

    def step(i, carry):
        even = lax.rem(i, 2) == 0
        u = lax.div(i, 2) + 1

        @pl.when(i == 3)
        def _():
            for n in (0, 1):
                hop_c(0, 1, n).wait_recv()
                hop_c(1, 2, n).start()

        for at, n in ((5, 3), (7, 2)):

            @pl.when(i == at)
            def _():
                hop_c(0, 2, n).wait_recv()
                hop_c(2, 1, n).start()

        @pl.when(i == 8)
        def _():
            for n in (3, 2):
                hop_c(0, 1, n).wait_recv()
            take(1)

        @pl.when(i == 14)
        def _():
            for n in (0, 1):
                hop_c(0, 2, n).wait_recv()
            take(2)
            for n in (0, 1):
                hop_c(1, 2, n).wait_recv()
            for n in (3, 2):
                hop_c(2, 1, n).wait_recv()
            take(3)
            for n in range(1, 2 * NZ):
                ss_copy(n).start()

        deep = ((u >= 8) & (u < 10)) | (u >= 12)

        @pl.when(even & (u < UNITS) & deep)
        def _():
            unit_deep(u)

        @pl.when(even & (u < UNITS) & jnp.logical_not(deep))
        def _():
            unit_wide(u)

        @pl.when(even & (u <= UNITS))
        def _():
            x_copy(u - 1).wait_recv()
            for h in range(2):
                own[2 * (u - 1) + h] = own[2 * (u - 1) + h] + xr[2 * (u - 1) + h].astype(f32)

        p = i - LAG * z

        @pl.when((p >= 0) & (p < CHUNKS))
        def _():
            @pl.when(z > 0)
            def _():
                up_copy(p).wait_recv()

            @pl.when(z < NZ - 1)
            def _():
                pout[p] = (own[p] + pin[p].astype(f32)).astype(bf16)
                up_copy(p).start()

        q = i - LAG * (NZ - 1 - z)

        @pl.when((q >= 0) & (q < CHUNKS))
        def _():
            @pl.when(z < NZ - 1)
            def _():
                down_copy(q).wait_recv()

            @pl.when(z > 0)
            def _():
                sout[q] = (own[q] + sin[q].astype(f32)).astype(bf16)
                down_copy(q).start()

        last = i - LAG * (NZ - 1)

        @pl.when(last == 16)
        def _():
            total = ss_own[...]
            for n in range(1, 2 * NZ):
                ss_copy(n).wait_recv()
                total = total + ss_in[n - 1]
            rinv[...] = lax.rsqrt(total * (1.0 / 8192.0) + epsilon)

        @pl.when((last == 17) | (last == 19))
        def _():
            f = lax.div(last - 17, 2)

            def put(j, v):
                tkv[f, xor2(c, j)] = v

            finish(f, put)
            for kk in range(2):
                me = (kv_col == c) & (k == kk)

                @pl.when(me)
                def _():
                    kv_copy(f, kk, True).start()

                @pl.when(jnp.logical_not(me))
                def _():
                    kv_copy(f, kk, False).start()

        @pl.when((last >= 25) & (last < CHUNKS) & (lax.rem(last, 2) == 1))
        def _():
            f = lax.div(last - 25, 2)

            def put(j, v):
                tq[f, k, j] = v

            finish(f + 2, put)
            t_copy(f).start()

        @pl.when(last == 24)
        def _():
            kv_prepare(0)

        @pl.when(last == 29)
        def _():
            kv_prepare(1)

        v = last - 28

        @pl.when((v >= 0) & (lax.rem(v, 2) == 0))
        def _():
            t_copy(lax.div(v, 2)).wait_recv()
            attend(lax.div(v, 2))

        return carry

    lax.fori_loop(0, CHUNKS + LAG * (NZ - 1) + 3, step, 0)

    for j in range(4):
        for kk in range(2):
            if j or kk:
                hop_a(j, kk).wait_send()
        t = xor2(c, j)

        @pl.when(t != z)
        def _():
            src, dst = hop_b(t, z)
            remote(src, dst, b_snd.at[t], b_rcv.at[z], dev(t, k, c)).wait_send()

    for n in range(NZ):
        hop_c(0, 1, n).wait_send()
        hop_c(0, 2, n).wait_send()
        if n < 2:
            hop_c(1, 2, n).wait_send()
        else:
            hop_c(2, 1, n).wait_send()

    def drain_units(u, carry):
        x_copy(u).wait_send()
        return carry

    lax.fori_loop(0, UNITS, drain_units, 0)

    def drain_chunks(i, carry):
        @pl.when(z < NZ - 1)
        def _():
            up_copy(i).wait_send()

        @pl.when(z > 0)
        def _():
            down_copy(i).wait_send()

        return carry

    lax.fori_loop(0, CHUNKS, drain_chunks, 0)
    for n in range(1, 2 * NZ):
        ss_copy(n).wait_send()
    for f in range(2):
        for kk in range(2):

            @pl.when(jnp.logical_not((kv_col == c) & (k == kk)))
            def _():
                kv_copy(f, kk, False).wait_send()

    def drain_heads(f, carry):
        t_copy(f).wait_send()
        return carry

    lax.fori_loop(0, 8, drain_heads, 0)


def square_form(token_ids, seq_lengths, embed_table, norm_gain, query_weight, kv_weight):
    bf16, f32 = jnp.bfloat16, jnp.float32
    vm = pltpu.VMEM
    dma = pltpu.SemaphoreType.DMA
    vspec = pl.BlockSpec(memory_space=pltpu.VMEM)
    aspec = pl.BlockSpec(memory_space=pltpu.HBM)
    return pl.pallas_call(
        fused,
        out_shape=pltpu.VMEM((TOK, 2048), bf16),
        in_specs=[vspec, pl.BlockSpec(memory_space=pltpu.SMEM), aspec, aspec, aspec, aspec, aspec],
        out_specs=vspec,
        scratch_shapes=[
            vm((64, 2048), bf16),
            vm((1, KD), f32),
            vm((4, HD // 2, SEQ), f32),
            vm((2560, KD), bf16),
            vm((128, KD), bf16),
            vm((VROWS, KD), bf16),
            vm((VROWS, KD), bf16),
            vm((CHUNKS, 128, 128), f32),
            vm((CHUNKS, 128, 128), bf16),
            vm((CHUNKS, 128, 128), bf16),
            vm((CHUNKS, 128, 128), bf16),
            vm((CHUNKS, 128, 128), bf16),
            vm((CHUNKS, 128, 128), bf16),
            vm((CHUNKS, 128, 128), bf16),
            vm((2 * NZ - 1, 8, 128), f32),
            vm((8, 128), f32),
            vm((8, 128), f32),
            vm((2, 4, 128, 128), bf16),
            vm((2, 2, 4, 128, 128), bf16),
            vm((8, 2, 4, 128, 128), bf16),
            vm((VROWS, TOK), bf16),
            vm((2, SEQ, SEQ), f32),
            vm((2, TOK, 128), bf16),
            vm((2, 128, TOK), bf16),
            dma((3,)),
            dma((20,)),
            dma((8,)), dma((8,)),
            dma((NZ,)), dma((NZ,)),
            dma((12,)), dma((12,)),
            dma((UNITS,)), dma((UNITS,)),
            dma((CHUNKS,)), dma((CHUNKS,)),
            dma((CHUNKS,)), dma((CHUNKS,)),
            dma((2 * NZ - 1,)), dma((2 * NZ - 1,)),
            dma((4,)), dma((4,)),
            dma((8,)), dma((8,)),
        ],
        cost_estimate=pl.CostEstimate(flops=6 * 10**9, bytes_accessed=8 * 10**6, transcendentals=2 * 10**6),
        compiler_params=pltpu.CompilerParams(
            collective_id=0, has_side_effects=True, vmem_limit_bytes=60 * 1024 * 1024
        ),
        name="fused",
    )(
        token_ids.reshape(1, TOK),
        seq_lengths,
        embed_table,
        norm_gain.reshape(1, -1),
        jnp.asarray(rope_constants()),
        query_weight,
        kv_weight,
    )


def solution(mesh):
    dp, tensor = mesh.shape["dp"], mesh.shape["tensor"]
    placed = (P("dp"), P("dp"), P("dp", "tensor"), P(), P("tensor", "dp"), P("tensor", "dp"))

    def on_device(*args):
        tokens, lengths, table, gain, qw, kvw = args
        square = (
            (dp, tensor) == (2 * NZ, 4)
            and tokens.shape == (TOK,)
            and lengths.shape == (2,)
            and table.shape == (64, 2048)
            and qw.shape == (2048, KD)
            and kvw.shape == (512, KD)
        )
        return square_form(*args) if square else general_form(*args)

    return jax.shard_map(
        on_device, mesh=mesh, in_specs=placed, out_specs=P("dp", "tensor"), check_vma=False
    )
```

```python
import functools
import math

import jax
import jax.numpy as jnp
import numpy as np
from jax import lax
from jax.experimental import pallas as pl
from jax.experimental.pallas import tpu as pltpu
from jax.sharding import PartitionSpec as P

HD = 128
HEADS = 64
KV_HEADS = 8
SEQ = 256
MESH = pl.DeviceIdType.MESH

epsilon = 1e-05
rope_base = 500000.0


def rope_tables(positions, head_size):
    halfway = head_size // 2
    frequencies = rope_base ** (-(jnp.arange(halfway, dtype=jnp.float32) * 2.0 / head_size))
    angles = positions.astype(jnp.float32)[:, None] * frequencies[None, :]
    return (jnp.cos(angles), jnp.sin(angles))


def rotate_last(values, cosine, sine_vals):
    halfway = values.shape[-1] // 2
    lower = values[..., :halfway]
    upper = values[..., halfway:]
    return jnp.concatenate(
        [lower * cosine - upper * sine_vals, upper * cosine + lower * sine_vals], axis=-1
    )


def general_form(token_ids, seq_lengths, embed_table, norm_gain, query_weight, kv_weight):
    tok_rows = token_ids.shape[0]
    tensor_index = lax.axis_index("tensor")
    heads_here = query_weight.shape[0] // HD
    group_size = HEADS // KV_HEADS
    kv_count = max(1, heads_here // group_size)
    per_group = heads_here // kv_count
    first_kv = tensor_index * heads_here // group_size
    rows = lax.all_gather(embed_table, "tensor", axis=1, tiled=True).astype(jnp.float32)
    mean_square = jnp.mean(rows * rows, axis=1, keepdims=True)
    normed_rows = (rows * lax.rsqrt(mean_square + epsilon) * norm_gain[None, :]).astype(jnp.bfloat16)
    normed = lax.all_to_all(normed_rows, "dp", split_axis=1, concat_axis=0, tiled=True)
    vocab_size = normed.shape[0]
    kv_grid = lax.all_gather(kv_weight, "tensor", axis=0, tiled=True).reshape(2, KV_HEADS, HD, -1)
    kv_rows = lax.dynamic_slice_in_dim(kv_grid, first_kv, kv_count, 1).reshape(2 * kv_count * HD, -1)
    weights = jnp.concatenate([query_weight, kv_rows], axis=0)
    partial = lax.dot_general(
        normed, weights, (((1,), (1,)), ((), ())), preferred_element_type=jnp.float32
    )
    summed = lax.psum_scatter(partial, "dp", scatter_dimension=0, tiled=True)
    table = lax.all_gather(summed.astype(jnp.bfloat16), "dp", axis=0, tiled=True)
    one_hot = (token_ids[:, None] == jnp.arange(vocab_size, dtype=jnp.int32)[None, :]).astype(
        jnp.bfloat16
    )
    picked = jnp.dot(one_hot, table, preferred_element_type=jnp.float32)
    q_width = heads_here * HD
    queries = picked[:, :q_width]
    seq_count = tok_rows // SEQ
    positions = jnp.arange(tok_rows, dtype=jnp.int32) % SEQ
    cosine, sine_vals = rope_tables(positions, HD)
    rot_queries = rotate_last(
        queries.reshape(tok_rows, heads_here, HD), cosine[:, None, :], sine_vals[:, None, :]
    ).astype(jnp.bfloat16)
    local = picked[:, q_width:].reshape(tok_rows, 2, kv_count, HD)
    rot_keys = rotate_last(
        local[:, 0], cosine[:, None, :], sine_vals[:, None, :]
    ).astype(jnp.bfloat16)
    query_grid = rot_queries.reshape(seq_count, SEQ, kv_count, per_group, HD)
    key_grid = rot_keys.reshape(seq_count, SEQ, kv_count, HD)
    value_grid = local[:, 1].astype(jnp.bfloat16).reshape(seq_count, SEQ, kv_count, HD)
    scores = jnp.einsum(
        "sqghd,skgd->sghqk", query_grid, key_grid, preferred_element_type=jnp.float32
    ) / math.sqrt(HD)
    slots = jnp.arange(SEQ, dtype=jnp.int32)
    causal = slots[None, :] <= slots[:, None]
    live = slots[None, :] < seq_lengths[:, None]
    allowed = causal[None, :, :] & live[:, None, :]
    scores = jnp.where(allowed[:, None, None, :, :], scores, -1e30)
    largest = jnp.max(scores, axis=-1, keepdims=True)
    exponent = jnp.exp(scores - largest)
    probs = (exponent / jnp.sum(exponent, axis=-1, keepdims=True)).astype(jnp.bfloat16)
    attended = jnp.einsum(
        "sghqk,skgd->sqghd", probs, value_grid, preferred_element_type=jnp.float32
    )
    return attended.astype(jnp.bfloat16).reshape(tok_rows, heads_here * HD)


NZ = 4
LAG = 5
UNITS = 20
CHUNKS = 2 * UNITS
KD = 1024
VROWS = 512
TOK = 512


def xor2(c, j):
    x, y = lax.rem(c, 2), lax.div(c, 2)
    if j & 1:
        x = 1 - x
    if j & 2:
        y = 1 - y
    return 2 * y + x


def chunk_of(f, j):
    if j == 0:
        return f
    later = jnp.where(f < 6, 0, jnp.where(f < 8, 1, 2))
    if j == 1:
        return f + jnp.where(f < 6, 10, 18 + 4 * later)
    return 16 + 2 * f + 2 * later + (j - 2)


def rope_constants():
    freq = rope_base ** (-(np.arange(HD // 2, dtype=np.float64) * 2.0 / HD))
    angle = freq[:, None] * np.arange(SEQ, dtype=np.float64)[None, :]
    scale = math.log2(math.e) / math.sqrt(HD)
    cos, sin = np.cos(angle), np.sin(angle)
    return np.stack([cos * scale, sin * scale, cos, sin]).astype(np.float32)


def fused(
    tok_hbm, len_hbm, emb_hbm, gain_hbm, rope_hbm, qw_hbm, kvw_hbm, out_ref,
    tok_ref, len_ref, emb_ref, gain_ref, rope,
    w, hop, ein, xin, own, xs, xr, pin, pout, sin, sout, ss_in, ss_own, rinv, tkv, kvt, tq,
    oh, bias, keys, vals,
    i_sem, w_sem, a_snd, a_rcv, b_snd, b_rcv, e_snd, e_rcv, x_snd, x_rcv, p_snd, p_rcv, s_snd, s_rcv,
    n_snd, n_rcv, kv_snd, kv_rcv, t_snd, t_rcv,
):
    f32, bf16 = jnp.float32, jnp.bfloat16
    d = lax.axis_index("dp")
    c = lax.axis_index("tensor")
    z, k = lax.div(d, 2), lax.rem(d, 2)

    def dev(zz, kk, cc):
        return (2 * zz + kk, cc)

    def remote(src, dst, snd, rcv, to):
        return pltpu.make_async_remote_copy(
            src_ref=src, dst_ref=dst, send_sem=snd, recv_sem=rcv, device_id=to, device_id_type=MESH
        )

    emb_copy = pltpu.make_async_copy(emb_hbm, emb_ref, i_sem.at[0])
    emb_copy.start()

    barrier = pltpu.get_barrier_semaphore()
    for dz in range(1, NZ):
        for kk in range(2):
            pl.semaphore_signal(
                barrier, inc=1, device_id=dev(lax.rem(z + dz, NZ), kk, c), device_id_type=MESH
            )
    for j in range(4):
        for kk in range(2):
            if j or kk:
                pl.semaphore_signal(
                    barrier, inc=1, device_id=dev(z, lax.rem(k + kk, 2), xor2(c, j)), device_id_type=MESH
                )

    emb_copy.wait()
    pl.semaphore_wait(barrier, 13)

    def hop_a(j, kk):
        c2, k2 = xor2(c, j), lax.rem(k + kk, 2)
        src = emb_ref.at[pl.ds(pl.multiple_of(16 * c2, 16), 16), pl.ds(pl.multiple_of(KD * k2, KD), KD)]
        dst = hop.at[pl.ds(pl.multiple_of(32 * c + 16 * k, 16), 16)]
        if j or kk:
            return remote(src, dst, a_snd.at[2 * j + kk], a_rcv.at[2 * j + kk], dev(z, k2, c2))
        return pltpu.make_async_copy(src, dst, a_rcv.at[0])

    for j, kk in ((0, 1), (0, 0), (1, 0), (1, 1), (2, 0), (2, 1), (3, 0), (3, 1)):
        hop_a(j, kk).start()

    tok_copy = pltpu.make_async_copy(tok_hbm, tok_ref, i_sem.at[3])
    tok_copy.start()
    len_copy = pltpu.make_async_copy(len_hbm, len_ref, i_sem.at[4])
    len_copy.start()
    rope_copy = pltpu.make_async_copy(rope_hbm, rope, i_sem.at[1])
    rope_copy.start()
    gain_copy = pltpu.make_async_copy(
        gain_hbm.at[:, pl.ds(pl.multiple_of(KD * d, KD), KD)], gain_ref, i_sem.at[2]
    )
    gain_copy.start()
    weight_copies = []
    for f in range(10):
        for side in range(2):
            kk = k if side == 0 else 1 - k
            if f < 2:
                src = kvw_hbm.at[pl.ds(pl.multiple_of((2 * kk + f) * 128, 128), 128)]
            else:
                src = qw_hbm.at[pl.ds(pl.multiple_of((f - 2) * 256 + kk * 128, 128), 128)]
            cp = pltpu.make_async_copy(src, w.at[pl.ds(f * 256 + side * 128, 128)], w_sem.at[2 * f + side])
            cp.start()
            weight_copies.append(cp)

    def hop_b(t, src_z):
        src = hop.at[pl.ds(pl.multiple_of(32 * t, 32), 32)]
        dst = ein.at[pl.ds(pl.multiple_of(32 * src_z, 32), 32)]
        return src, dst

    def pass_on(j):
        for kk in range(2):
            cp = hop_a(j, kk)
            if j or kk:
                cp.wait_recv()
            else:
                cp.wait()
        t = xor2(c, j)
        src, dst = hop_b(t, z)

        @pl.when(t != z)
        def _():
            remote(src, dst, b_snd.at[t], b_rcv.at[z], dev(t, k, c)).start()

        @pl.when(t == z)
        def _():
            pltpu.make_async_copy(src, dst, b_rcv.at[z]).start()

    pass_on(0)
    spot = lax.broadcasted_iota(jnp.int32, (128, TOK), 0)
    base = (spot >> 4) * 64 + (spot & 15)
    tok_copy.wait()
    len_copy.wait()
    toks = tok_ref[...]
    for j in range(4):
        hit = (base + 16 * xor2(c, j)) == toks
        oh[pl.ds(128 * j, 128), :] = jnp.where(hit, 1.0, 0.0).astype(bf16)
    pass_on(1)
    pass_on(2)
    pass_on(3)
    kpos = lax.broadcasted_iota(jnp.int32, (SEQ, SEQ), 0)
    qpos = lax.broadcasted_iota(jnp.int32, (SEQ, SEQ), 1)
    for s in range(2):
        good = (kpos <= qpos) & (kpos < len_ref[s])
        bias[s] = jnp.where(good, 0.0, -1e30)
    ss_own[...] = jnp.zeros_like(ss_own)

    @pl.when(z == 0)
    def _():
        pin[...] = jnp.zeros_like(pin)

    @pl.when(z == NZ - 1)
    def _():
        sin[...] = jnp.zeros_like(sin)

    gain_copy.wait()
    rope_copy.wait()
    for cp in weight_copies:
        cp.wait()

    def piece(n):
        return pl.multiple_of(32 * lax.rem(z + n, NZ), 32)

    def hop_c(place, to, n):
        src = ein.at[pl.ds(128 * place + piece(n), 32)]
        dst = ein.at[pl.ds(128 * (place + to) + piece(n), 32)]
        i = 4 * (place + to - 1) + n
        return remote(src, dst, e_snd.at[i], e_rcv.at[i], dev(z, k, xor2(c, to)))

    for n in (0, 1, 3, 2):
        src, dst = hop_b(lax.rem(z + n, NZ), lax.rem(z + n, NZ))
        pltpu.make_async_copy(src, dst, b_rcv.at[lax.rem(z + n, NZ)]).wait()
        hop_c(0, 1, n).start()
        hop_c(0, 2, n).start()
        fresh = pl.ds(piece(n), 32)
        xin[fresh, :] = (ein[fresh, :].astype(f32) * gain_ref[...]).astype(bf16)

    ones = jnp.ones((8, KD), bf16)
    nt = (((1,), (1,)), ((), ()))

    def take(j):
        raw = ein[pl.ds(128 * j, 128), :].astype(f32)
        xin[pl.ds(128 * j, 128), :] = (raw * gain_ref[...]).astype(bf16)

    def square(j):
        raw = ein[pl.ds(128 * j, 128), :].astype(f32)
        squares = (raw * raw).astype(bf16)
        ss = lax.dot_general(ones, squares, nt, preferred_element_type=f32)
        ss_own[pl.ds(j, 1), :] = ss[0:1, :]

    def x_copy(u):
        return remote(
            xs.at[pl.ds(2 * u, 2)], xr.at[pl.ds(2 * u, 2)], x_snd.at[u], x_rcv.at[u], dev(z, 1 - k, c)
        )

    def unit_wide(u):
        place = jnp.where(u < 5, 0, 1)
        f0 = jnp.where(u < 5, 2 * u, jnp.where(u < 8, 2 * (u - 5), jnp.where(u < 16, 6, 8)))
        x = xin[pl.ds(pl.multiple_of(128 * place, 128), 128), :]
        res = lax.dot_general(
            w[pl.ds(pl.multiple_of(256 * f0, 256), 512), :], x, nt, preferred_element_type=f32
        )
        for h in range(2):
            own[2 * u + h] = res[256 * h : 256 * h + 128]
            xs[2 * u + h] = res[256 * h + 128 : 256 * h + 256].astype(bf16)
        x_copy(u).start()

    def unit_deep(u):
        f = u - jnp.where(u < 14, 8, jnp.where(u < 17, 9, 10))
        res = lax.dot_general(
            w[pl.ds(pl.multiple_of(256 * f, 256), 256), :], xin[256:512, :], nt, preferred_element_type=f32
        )
        for h in range(2):
            own[2 * u + h] = res[:128, 128 * h : 128 * h + 128]
            xs[2 * u + h] = res[128:, 128 * h : 128 * h + 128].astype(bf16)
        x_copy(u).start()

    def up_copy(u):
        both = pl.ds(2 * u, 2)
        return remote(pout.at[both], pin.at[both], p_snd.at[u], p_rcv.at[u], dev(lax.rem(z + 1, NZ), k, c))

    def down_copy(u):
        both = pl.ds(2 * u, 2)
        return remote(
            sout.at[both], sin.at[both], s_snd.at[u], s_rcv.at[u], dev(lax.rem(z + NZ - 1, NZ), k, c)
        )

    def move_up(p):
        u = lax.div(p, 2)

        @pl.when((p >= 0) & (u < UNITS) & (lax.rem(p, 2) == 0))
        def _():
            @pl.when(z > 0)
            def _():
                up_copy(u).wait_recv()

            @pl.when(z < NZ - 1)
            def _():
                for h in range(2):
                    pout[2 * u + h] = (own[2 * u + h] + pin[2 * u + h].astype(f32)).astype(bf16)
                up_copy(u).start()

    def move_down(q):
        u = lax.div(q, 2)

        @pl.when((q >= 0) & (u < UNITS) & (lax.rem(q, 2) == 0))
        def _():
            @pl.when(z < NZ - 1)
            def _():
                down_copy(u).wait_recv()

            @pl.when(z > 0)
            def _():
                for h in range(2):
                    sout[2 * u + h] = (own[2 * u + h] + sin[2 * u + h].astype(f32)).astype(bf16)
                down_copy(u).start()

    def ss_copy(i):
        other = lax.rem(d + i, 2 * NZ)
        return remote(ss_own, ss_in.at[i - 1], n_snd.at[i - 1], n_rcv.at[i - 1], (other, c))

    def t_copy(f):
        return remote(tq.at[f, k], tq.at[f, k], t_snd.at[f], t_rcv.at[f], dev(z, 1 - k, c))

    kv_col = 2 * lax.rem(c, 2) + k
    kv_kind = lax.div(c, 2)

    def kv_copy(f, kk, local):
        dst = kvt.at[kv_kind, f]
        rcv = kv_rcv.at[2 * kv_kind + f]
        if local:
            return pltpu.make_async_copy(tkv.at[f], dst, rcv)
        return remote(tkv.at[f], dst, kv_snd.at[2 * f + kk], rcv, dev(z, kk, kv_col))

    def finish(f, put):
        for j in range(4):
            i = chunk_of(f, j)
            total = own[i] + pin[i].astype(f32) + sin[i].astype(f32)
            put(j, (total * rinv[pl.ds(j, 1), :]).astype(bf16))

    def kv_prepare(g):
        for kind in range(2):
            pltpu.make_async_copy(tkv.at[0], kvt.at[kind, g], kv_rcv.at[2 * kind + g]).wait()
        picked = []
        for kind in range(2):
            acc = jnp.zeros((128, TOK), f32)
            for a in range(4):
                ohg = oh[pl.ds(pl.multiple_of(128 * xor2(c, a), 128), 128), :]
                acc = acc + jnp.dot(kvt[kind, g, a], ohg, preferred_element_type=f32)
            picked.append(acc)
        lo, hi = picked[0][:64], picked[0][64:]
        cos = jnp.concatenate([rope[2]] * 2, axis=1)
        sine = jnp.concatenate([rope[3]] * 2, axis=1)
        rot = jnp.concatenate([lo * cos - hi * sine, hi * cos + lo * sine], axis=0)
        keys[g] = rot.T.astype(bf16)
        vals[g] = picked[1].astype(bf16)

    def attend(f):
        g = lax.div(f, 4)
        table = jnp.concatenate(
            [jnp.concatenate([tq[f, kk, j] for j in range(4)], axis=1) for kk in range(2)], axis=0
        )
        picked = jnp.dot(table, oh[...], preferred_element_type=f32)
        cos = jnp.concatenate([rope[0]] * 2, axis=1)
        sine = jnp.concatenate([rope[1]] * 2, axis=1)
        q = []
        for kk in range(2):
            lo, hi = picked[128 * kk : 128 * kk + 64], picked[128 * kk + 64 : 128 * kk + 128]
            q.append(jnp.concatenate([lo * cos - hi * sine, hi * cos + lo * sine], axis=0).astype(bf16))
        blocks = [(s, b) for s in range(2) for b in range(2)]
        scores = []
        for s, b in blocks:
            at = SEQ * s + 128 * b
            both = jnp.concatenate([v[:, at : at + 128] for v in q], axis=1)
            rows = keys[g, pl.ds(SEQ * s, 128 * (b + 1)), :]
            scores.append(jnp.dot(rows, both, preferred_element_type=f32))
        sums = []
        for (s, b), sc in zip(blocks, scores):
            n = 128 * (b + 1)
            es, dens = [], []
            for kk in range(2):
                x = sc[:, 128 * kk : 128 * kk + 128] + bias[s, :n, 128 * b : 128 * b + 128]
                e = jnp.exp2(x - jnp.max(x, axis=0, keepdims=True))
                dens.append(jnp.sum(e, axis=0, keepdims=True))
                es.append(e.astype(bf16))
            o = jnp.dot(
                vals[g, :, pl.ds(SEQ * s, n)], jnp.concatenate(es, axis=1), preferred_element_type=f32
            )
            sums.append((o, dens))
        for (s, b), (o, dens) in zip(blocks, sums):
            for kk in range(2):
                part = o[:, 128 * kk : 128 * kk + 128] * (1.0 / dens[kk])
                at = pl.multiple_of(256 * f + 128 * kk, 128)
                out_ref[pl.ds(SEQ * s + 128 * b, 128), pl.ds(at, 128)] = part.T.astype(bf16)

    unit_wide(jnp.int32(0))

    def step(i, carry):
        even = lax.rem(i, 2) == 0
        u = lax.div(i, 2) + 1

        @pl.when(i == 4)
        def _():
            for n in (0, 1):
                hop_c(0, 1, n).wait_recv()
                hop_c(1, 2, n).start()

        for at, n in ((6, 3), (8, 2)):

            @pl.when(i == at)
            def _():
                hop_c(0, 2, n).wait_recv()
                hop_c(2, 1, n).start()

        @pl.when(i == 8)
        def _():
            for n in (3, 2):
                hop_c(0, 1, n).wait_recv()
            take(1)

        @pl.when(i == 14)
        def _():
            for n in (0, 1):
                hop_c(0, 2, n).wait_recv()
            take(2)
            for n in (0, 1):
                hop_c(1, 2, n).wait_recv()
            for n in (3, 2):
                hop_c(2, 1, n).wait_recv()
            take(3)

        @pl.when(i == 15)
        def _():
            for j in range(4):
                square(j)
            for n in range(1, 2 * NZ):
                ss_copy(n).start()

        deep = (u >= 8) & (u != 14) & (u != 17)

        @pl.when(even & (u < UNITS) & deep)
        def _():
            unit_deep(u)

        @pl.when(even & (u < UNITS) & jnp.logical_not(deep))
        def _():
            unit_wide(u)

        @pl.when(even & (u <= UNITS))
        def _():
            x_copy(u - 1).wait_recv()
            for h in range(2):
                own[2 * (u - 1) + h] = own[2 * (u - 1) + h] + xr[2 * (u - 1) + h].astype(f32)

        @pl.when(z < NZ // 2)
        def _():
            move_up(i - LAG * z - k)
            move_down(i - LAG * (NZ - 1 - z) - k)

        @pl.when(z >= NZ // 2)
        def _():
            move_down(i - LAG * (NZ - 1 - z) - k)
            move_up(i - LAG * z - k)

        last = i - LAG * (NZ - 1)

        @pl.when(last == 16)
        def _():
            total = ss_own[...]
            for n in range(1, 2 * NZ):
                ss_copy(n).wait_recv()
                total = total + ss_in[n - 1]
            rinv[...] = lax.rsqrt(total * (1.0 / 8192.0) + epsilon)

        @pl.when((last == 17) | (last == 19))
        def _():
            f = lax.div(last - 17, 2)

            def put(j, v):
                tkv[f, xor2(c, j)] = v

            finish(f, put)
            for kk in range(2):
                me = (kv_col == c) & (k == kk)

                @pl.when(me)
                def _():
                    kv_copy(f, kk, True).start()

                @pl.when(jnp.logical_not(me))
                def _():
                    kv_copy(f, kk, False).start()

        gap = (last == 29) | (last == 35)

        @pl.when((last >= 21) & (last < CHUNKS) & (lax.rem(last, 2) == 1) & jnp.logical_not(gap))
        def _():
            f = lax.div(last - jnp.where(last < 29, 21, jnp.where(last < 35, 23, 25)), 2)

            def put(j, v):
                tq[f, k, j] = v

            finish(f + 2, put)
            t_copy(f).start()

        @pl.when(last == 24)
        def _():
            kv_prepare(0)

        @pl.when(last == 30)
        def _():
            kv_prepare(1)

        w0 = last - 25
        f_now = lax.div(w0, 2) - jnp.where(last < 37, 0, 1)

        @pl.when((w0 >= 0) & (lax.rem(w0, 2) == 0) & (last != 37))
        def _():
            t_copy(f_now).wait_recv()
            attend(f_now)

        return carry

    lax.fori_loop(0, CHUNKS + LAG * (NZ - 1) + 2, step, 0)

    for j in range(4):
        for kk in range(2):
            if j or kk:
                hop_a(j, kk).wait_send()
        t = xor2(c, j)

        @pl.when(t != z)
        def _():
            src, dst = hop_b(t, z)
            remote(src, dst, b_snd.at[t], b_rcv.at[z], dev(t, k, c)).wait_send()

    for n in range(NZ):
        hop_c(0, 1, n).wait_send()
        hop_c(0, 2, n).wait_send()
        if n < 2:
            hop_c(1, 2, n).wait_send()
        else:
            hop_c(2, 1, n).wait_send()

    def drain_units(u, carry):
        x_copy(u).wait_send()

        @pl.when(z < NZ - 1)
        def _():
            up_copy(u).wait_send()

        @pl.when(z > 0)
        def _():
            down_copy(u).wait_send()

        return carry

    lax.fori_loop(0, UNITS, drain_units, 0)
    for n in range(1, 2 * NZ):
        ss_copy(n).wait_send()
    for f in range(2):
        for kk in range(2):

            @pl.when(jnp.logical_not((kv_col == c) & (k == kk)))
            def _():
                kv_copy(f, kk, False).wait_send()

    def drain_heads(f, carry):
        t_copy(f).wait_send()
        return carry

    lax.fori_loop(0, 8, drain_heads, 0)


def square_form(token_ids, seq_lengths, embed_table, norm_gain, query_weight, kv_weight):
    bf16, f32 = jnp.bfloat16, jnp.float32
    vm = pltpu.VMEM
    dma = pltpu.SemaphoreType.DMA
    vspec = pl.BlockSpec(memory_space=pltpu.VMEM)
    aspec = pl.BlockSpec(memory_space=pltpu.HBM)
    return pl.pallas_call(
        fused,
        out_shape=pltpu.VMEM((TOK, 2048), bf16),
        in_specs=[aspec] * 7,
        out_specs=vspec,
        scratch_shapes=[
            vm((1, TOK), jnp.int32),
            pltpu.SMEM((2,), jnp.int32),
            vm((64, 2048), bf16),
            vm((1, KD), f32),
            vm((4, HD // 2, SEQ), f32),
            vm((2560, KD), bf16),
            vm((128, KD), bf16),
            vm((VROWS, KD), bf16),
            vm((VROWS, KD), bf16),
            vm((CHUNKS, 128, 128), f32),
            vm((CHUNKS, 128, 128), bf16),
            vm((CHUNKS, 128, 128), bf16),
            vm((CHUNKS, 128, 128), bf16),
            vm((CHUNKS, 128, 128), bf16),
            vm((CHUNKS, 128, 128), bf16),
            vm((CHUNKS, 128, 128), bf16),
            vm((2 * NZ - 1, 8, 128), f32),
            vm((8, 128), f32),
            vm((8, 128), f32),
            vm((2, 4, 128, 128), bf16),
            vm((2, 2, 4, 128, 128), bf16),
            vm((8, 2, 4, 128, 128), bf16),
            vm((VROWS, TOK), bf16),
            vm((2, SEQ, SEQ), f32),
            vm((2, TOK, 128), bf16),
            vm((2, 128, TOK), bf16),
            dma((5,)),
            dma((20,)),
            dma((8,)), dma((8,)),
            dma((NZ,)), dma((NZ,)),
            dma((12,)), dma((12,)),
            dma((UNITS,)), dma((UNITS,)),
            dma((UNITS,)), dma((UNITS,)),
            dma((UNITS,)), dma((UNITS,)),
            dma((2 * NZ - 1,)), dma((2 * NZ - 1,)),
            dma((4,)), dma((4,)),
            dma((8,)), dma((8,)),
        ],
        cost_estimate=pl.CostEstimate(flops=6 * 10**9, bytes_accessed=8 * 10**6, transcendentals=2 * 10**6),
        compiler_params=pltpu.CompilerParams(
            collective_id=0, has_side_effects=True, vmem_limit_bytes=60 * 1024 * 1024
        ),
        name="fused",
    )(
        token_ids.reshape(1, TOK),
        seq_lengths,
        embed_table,
        norm_gain.reshape(1, -1),
        jnp.asarray(rope_constants()),
        query_weight,
        kv_weight,
    )


def solution(mesh):
    dp, tensor = mesh.shape["dp"], mesh.shape["tensor"]
    placed = (P("dp"), P("dp"), P("dp", "tensor"), P(), P("tensor", "dp"), P("tensor", "dp"))

    def on_device(*args):
        tokens, lengths, table, gain, qw, kvw = args
        square = (
            (dp, tensor) == (2 * NZ, 4)
            and tokens.shape == (TOK,)
            and lengths.shape == (2,)
            and table.shape == (64, 2048)
            and qw.shape == (2048, KD)
            and kvw.shape == (512, KD)
        )
        return square_form(*args) if square else general_form(*args)

    return jax.shard_map(
        on_device, mesh=mesh, in_specs=placed, out_specs=P("dp", "tensor"), check_vma=False
    )
```

```python
import functools
import math

import jax
import jax.numpy as jnp
import numpy as np
from jax import lax
from jax.experimental import pallas as pl
from jax.experimental.pallas import tpu as pltpu
from jax.sharding import PartitionSpec as P

HD = 128
HEADS = 64
KV_HEADS = 8
SEQ = 256
MESH = pl.DeviceIdType.MESH

epsilon = 1e-05
rope_base = 500000.0


def rope_tables(positions, head_size):
    halfway = head_size // 2
    frequencies = rope_base ** (-(jnp.arange(halfway, dtype=jnp.float32) * 2.0 / head_size))
    angles = positions.astype(jnp.float32)[:, None] * frequencies[None, :]
    return (jnp.cos(angles), jnp.sin(angles))


def rotate_last(values, cosine, sine_vals):
    halfway = values.shape[-1] // 2
    lower = values[..., :halfway]
    upper = values[..., halfway:]
    return jnp.concatenate(
        [lower * cosine - upper * sine_vals, upper * cosine + lower * sine_vals], axis=-1
    )


def general_form(token_ids, seq_lengths, embed_table, norm_gain, query_weight, kv_weight):
    tok_rows = token_ids.shape[0]
    tensor_index = lax.axis_index("tensor")
    heads_here = query_weight.shape[0] // HD
    group_size = HEADS // KV_HEADS
    kv_count = max(1, heads_here // group_size)
    per_group = heads_here // kv_count
    first_kv = tensor_index * heads_here // group_size
    rows = lax.all_gather(embed_table, "tensor", axis=1, tiled=True).astype(jnp.float32)
    mean_square = jnp.mean(rows * rows, axis=1, keepdims=True)
    normed_rows = (rows * lax.rsqrt(mean_square + epsilon) * norm_gain[None, :]).astype(jnp.bfloat16)
    normed = lax.all_to_all(normed_rows, "dp", split_axis=1, concat_axis=0, tiled=True)
    vocab_size = normed.shape[0]
    kv_grid = lax.all_gather(kv_weight, "tensor", axis=0, tiled=True).reshape(2, KV_HEADS, HD, -1)
    kv_rows = lax.dynamic_slice_in_dim(kv_grid, first_kv, kv_count, 1).reshape(2 * kv_count * HD, -1)
    weights = jnp.concatenate([query_weight, kv_rows], axis=0)
    partial = lax.dot_general(
        normed, weights, (((1,), (1,)), ((), ())), preferred_element_type=jnp.float32
    )
    summed = lax.psum_scatter(partial, "dp", scatter_dimension=0, tiled=True)
    table = lax.all_gather(summed.astype(jnp.bfloat16), "dp", axis=0, tiled=True)
    one_hot = (token_ids[:, None] == jnp.arange(vocab_size, dtype=jnp.int32)[None, :]).astype(
        jnp.bfloat16
    )
    picked = jnp.dot(one_hot, table, preferred_element_type=jnp.float32)
    q_width = heads_here * HD
    queries = picked[:, :q_width]
    seq_count = tok_rows // SEQ
    positions = jnp.arange(tok_rows, dtype=jnp.int32) % SEQ
    cosine, sine_vals = rope_tables(positions, HD)
    rot_queries = rotate_last(
        queries.reshape(tok_rows, heads_here, HD), cosine[:, None, :], sine_vals[:, None, :]
    ).astype(jnp.bfloat16)
    local = picked[:, q_width:].reshape(tok_rows, 2, kv_count, HD)
    rot_keys = rotate_last(
        local[:, 0], cosine[:, None, :], sine_vals[:, None, :]
    ).astype(jnp.bfloat16)
    query_grid = rot_queries.reshape(seq_count, SEQ, kv_count, per_group, HD)
    key_grid = rot_keys.reshape(seq_count, SEQ, kv_count, HD)
    value_grid = local[:, 1].astype(jnp.bfloat16).reshape(seq_count, SEQ, kv_count, HD)
    scores = jnp.einsum(
        "sqghd,skgd->sghqk", query_grid, key_grid, preferred_element_type=jnp.float32
    ) / math.sqrt(HD)
    slots = jnp.arange(SEQ, dtype=jnp.int32)
    causal = slots[None, :] <= slots[:, None]
    live = slots[None, :] < seq_lengths[:, None]
    allowed = causal[None, :, :] & live[:, None, :]
    scores = jnp.where(allowed[:, None, None, :, :], scores, -1e30)
    largest = jnp.max(scores, axis=-1, keepdims=True)
    exponent = jnp.exp(scores - largest)
    probs = (exponent / jnp.sum(exponent, axis=-1, keepdims=True)).astype(jnp.bfloat16)
    attended = jnp.einsum(
        "sghqk,skgd->sqghd", probs, value_grid, preferred_element_type=jnp.float32
    )
    return attended.astype(jnp.bfloat16).reshape(tok_rows, heads_here * HD)


NZ = 4
LAG = 6
UNITS = 20
CHUNKS = 2 * UNITS
KD = 1024
VROWS = 512
TOK = 512


def xor2(c, j):
    x, y = lax.rem(c, 2), lax.div(c, 2)
    if j & 1:
        x = 1 - x
    if j & 2:
        y = 1 - y
    return 2 * y + x


def chunk_of(f, j):
    if j == 0:
        return f
    later = jnp.where(f < 6, 0, jnp.where(f < 8, 1, 2))
    if j == 1:
        return f + jnp.where(f < 6, 10, 18 + 4 * later)
    return 16 + 2 * f + 2 * later + (j - 2)


def rope_constants():
    freq = rope_base ** (-(np.arange(HD // 2, dtype=np.float64) * 2.0 / HD))
    angle = freq[:, None] * np.arange(SEQ, dtype=np.float64)[None, :]
    scale = math.log2(math.e) / math.sqrt(HD)
    cos, sin = np.cos(angle), np.sin(angle)
    return np.stack([cos * scale, sin * scale, cos, sin]).astype(np.float32)


def fused(
    tok_hbm, len_hbm, emb_hbm, gain_hbm, rope_hbm, qw_hbm, kvw_hbm, out_ref,
    tok_ref, len_ref, emb_ref, gain_ref, rope,
    w, hop, ein, xin, own, xs, xr, pin, pout, sin, sout, ss_in, ss_own, rinv, tkv, kvt, tq,
    oh, bias, keys, vals,
    i_sem, w_sem, a_snd, a_rcv, b_snd, b_rcv, e_snd, e_rcv, x_snd, x_rcv, p_snd, p_rcv, s_snd, s_rcv,
    n_snd, n_rcv, kv_snd, kv_rcv, t_snd, t_rcv,
):
    f32, bf16 = jnp.float32, jnp.bfloat16
    d = lax.axis_index("dp")
    c = lax.axis_index("tensor")
    z, k = lax.div(d, 2), lax.rem(d, 2)

    def dev(zz, kk, cc):
        return (2 * zz + kk, cc)

    def remote(src, dst, snd, rcv, to):
        return pltpu.make_async_remote_copy(
            src_ref=src, dst_ref=dst, send_sem=snd, recv_sem=rcv, device_id=to, device_id_type=MESH
        )

    emb_copy = pltpu.make_async_copy(emb_hbm, emb_ref, i_sem.at[0])
    emb_copy.start()

    barrier = pltpu.get_barrier_semaphore()
    for dz in range(1, NZ):
        for kk in range(2):
            pl.semaphore_signal(
                barrier, inc=1, device_id=dev(lax.rem(z + dz, NZ), kk, c), device_id_type=MESH
            )
    for j in range(4):
        for kk in range(2):
            if j or kk:
                pl.semaphore_signal(
                    barrier, inc=1, device_id=dev(z, lax.rem(k + kk, 2), xor2(c, j)), device_id_type=MESH
                )

    emb_copy.wait()
    pl.semaphore_wait(barrier, 13)

    def hop_a(j, kk):
        c2, k2 = xor2(c, j), lax.rem(k + kk, 2)
        src = emb_ref.at[pl.ds(pl.multiple_of(16 * c2, 16), 16), pl.ds(pl.multiple_of(KD * k2, KD), KD)]
        dst = hop.at[pl.ds(pl.multiple_of(32 * c + 16 * k, 16), 16)]
        if j or kk:
            return remote(src, dst, a_snd.at[2 * j + kk], a_rcv.at[2 * j + kk], dev(z, k2, c2))
        return pltpu.make_async_copy(src, dst, a_rcv.at[0])

    hop_a(0, 1).start()
    hop_a(0, 0).start()
    for rel in range(2):
        for j in (1, 2, 3):
            hop_a(j, rel).start()

    tok_copy = pltpu.make_async_copy(tok_hbm, tok_ref, i_sem.at[3])
    tok_copy.start()
    len_copy = pltpu.make_async_copy(len_hbm, len_ref, i_sem.at[4])
    len_copy.start()
    rope_copy = pltpu.make_async_copy(rope_hbm, rope, i_sem.at[1])
    rope_copy.start()
    gain_copy = pltpu.make_async_copy(
        gain_hbm.at[:, pl.ds(pl.multiple_of(KD * d, KD), KD)], gain_ref, i_sem.at[2]
    )
    gain_copy.start()
    weight_copies = []
    for f in range(10):
        for side in range(2):
            kk = k if side == 0 else 1 - k
            if f < 2:
                src = kvw_hbm.at[pl.ds(pl.multiple_of((2 * kk + f) * 128, 128), 128)]
            else:
                src = qw_hbm.at[pl.ds(pl.multiple_of((f - 2) * 256 + kk * 128, 128), 128)]
            cp = pltpu.make_async_copy(src, w.at[pl.ds(f * 256 + side * 128, 128)], w_sem.at[2 * f + side])
            cp.start()
            weight_copies.append(cp)

    def hop_b(t, src_z, kk):
        src = hop.at[pl.ds(pl.multiple_of(32 * t + 16 * kk, 16), 16)]
        dst = ein.at[pl.ds(pl.multiple_of(32 * src_z + 16 * kk, 16), 16)]
        return src, dst

    def pass_on(j, rel):
        t = xor2(c, j)
        cp = hop_a(j, rel)
        if j or rel:
            cp.wait_recv()
        else:
            cp.wait()
        kk = lax.rem(k + rel, 2)
        src, dst = hop_b(t, z, kk)

        @pl.when(t != z)
        def _():
            remote(src, dst, b_snd.at[2 * t + kk], b_rcv.at[2 * z + kk], dev(t, k, c)).start()

        @pl.when(t == z)
        def _():
            pltpu.make_async_copy(src, dst, b_rcv.at[2 * z + kk]).start()

    pass_on(0, 0)
    pass_on(0, 1)
    spot = lax.broadcasted_iota(jnp.int32, (128, TOK), 0)
    base = (spot >> 4) * 64 + (spot & 15)
    tok_copy.wait()
    len_copy.wait()
    toks = tok_ref[...]
    for j in range(4):
        hit = (base + 16 * xor2(c, j)) == toks
        oh[pl.ds(128 * j, 128), :] = jnp.where(hit, 1.0, 0.0).astype(bf16)
    for rel in range(2):
        for j in (1, 2, 3):
            pass_on(j, rel)
    kpos = lax.broadcasted_iota(jnp.int32, (SEQ, SEQ), 0)
    qpos = lax.broadcasted_iota(jnp.int32, (SEQ, SEQ), 1)
    for s in range(2):
        good = (kpos <= qpos) & (kpos < len_ref[s])
        bias[s] = jnp.where(good, 0.0, -1e30)
    ss_own[...] = jnp.zeros_like(ss_own)

    @pl.when(z == 0)
    def _():
        pin[...] = jnp.zeros_like(pin)

    @pl.when(z == NZ - 1)
    def _():
        sin[...] = jnp.zeros_like(sin)

    gain_copy.wait()
    rope_copy.wait()
    for cp in weight_copies:
        cp.wait()

    def piece(n):
        return pl.multiple_of(32 * lax.rem(z + n, NZ), 32)

    def hop_c(place, to, n):
        src = ein.at[pl.ds(128 * place + piece(n), 32)]
        dst = ein.at[pl.ds(128 * (place + to) + piece(n), 32)]
        i = 4 * (place + to - 1) + n
        return remote(src, dst, e_snd.at[i], e_rcv.at[i], dev(z, k, xor2(c, to)))

    for n in (0, 1, 3, 2):
        from_z = lax.rem(z + n, NZ)
        for kk in range(2):
            src, dst = hop_b(from_z, from_z, kk)
            pltpu.make_async_copy(src, dst, b_rcv.at[2 * from_z + kk]).wait()
        hop_c(0, 1, n).start()
        hop_c(0, 2, n).start()
        fresh = pl.ds(piece(n), 32)
        xin[fresh, :] = (ein[fresh, :].astype(f32) * gain_ref[...]).astype(bf16)

    ones = jnp.ones((8, KD), bf16)
    nt = (((1,), (1,)), ((), ()))

    def take(j):
        raw = ein[pl.ds(128 * j, 128), :].astype(f32)
        xin[pl.ds(128 * j, 128), :] = (raw * gain_ref[...]).astype(bf16)

    def square(j):
        raw = ein[pl.ds(128 * j, 128), :].astype(f32)
        squares = (raw * raw).astype(bf16)
        ss = lax.dot_general(ones, squares, nt, preferred_element_type=f32)
        ss_own[pl.ds(j, 1), :] = ss[0:1, :]

    def x_copy(u):
        return remote(
            xs.at[pl.ds(2 * u, 2)], xr.at[pl.ds(2 * u, 2)], x_snd.at[u], x_rcv.at[u], dev(z, 1 - k, c)
        )

    def unit_wide(u):
        place = jnp.where(u < 5, 0, 1)
        f0 = jnp.where(u < 5, 2 * u, jnp.where(u < 8, 2 * (u - 5), jnp.where(u < 16, 6, 8)))
        x = xin[pl.ds(pl.multiple_of(128 * place, 128), 128), :]
        res = lax.dot_general(
            w[pl.ds(pl.multiple_of(256 * f0, 256), 512), :], x, nt, preferred_element_type=f32
        )
        for h in range(2):
            own[2 * u + h] = res[256 * h : 256 * h + 128]
            xs[2 * u + h] = res[256 * h + 128 : 256 * h + 256].astype(bf16)
        x_copy(u).start()

    def unit_deep(u):
        f = u - jnp.where(u < 14, 8, jnp.where(u < 17, 9, 10))
        res = lax.dot_general(
            w[pl.ds(pl.multiple_of(256 * f, 256), 256), :], xin[256:512, :], nt, preferred_element_type=f32
        )
        for h in range(2):
            own[2 * u + h] = res[:128, 128 * h : 128 * h + 128]
            xs[2 * u + h] = res[128:, 128 * h : 128 * h + 128].astype(bf16)
        x_copy(u).start()

    def up_copy(u):
        both = pl.ds(2 * u, 2)
        return remote(pout.at[both], pin.at[both], p_snd.at[u], p_rcv.at[u], dev(lax.rem(z + 1, NZ), k, c))

    def down_copy(u):
        both = pl.ds(2 * u, 2)
        return remote(
            sout.at[both], sin.at[both], s_snd.at[u], s_rcv.at[u], dev(lax.rem(z + NZ - 1, NZ), k, c)
        )

    def move_up(p):
        u = lax.div(p, 2)

        @pl.when((p >= 0) & (u < UNITS) & (lax.rem(p, 2) == 0))
        def _():
            @pl.when(z > 0)
            def _():
                up_copy(u).wait_recv()

            @pl.when(z < NZ - 1)
            def _():
                for h in range(2):
                    pout[2 * u + h] = (own[2 * u + h] + pin[2 * u + h].astype(f32)).astype(bf16)
                up_copy(u).start()

    def move_down(q):
        u = lax.div(q, 2)

        @pl.when((q >= 0) & (u < UNITS) & (lax.rem(q, 2) == 0))
        def _():
            @pl.when(z < NZ - 1)
            def _():
                down_copy(u).wait_recv()

            @pl.when(z > 0)
            def _():
                for h in range(2):
                    sout[2 * u + h] = (own[2 * u + h] + sin[2 * u + h].astype(f32)).astype(bf16)
                down_copy(u).start()

    def ss_copy(i):
        other = lax.rem(d + i, 2 * NZ)
        return remote(ss_own, ss_in.at[i - 1], n_snd.at[i - 1], n_rcv.at[i - 1], (other, c))

    def t_copy(f):
        return remote(tq.at[f, k], tq.at[f, k], t_snd.at[f], t_rcv.at[f], dev(z, 1 - k, c))

    kv_col = 2 * lax.rem(c, 2) + k
    kv_kind = lax.div(c, 2)

    def kv_copy(f, kk, local):
        dst = kvt.at[kv_kind, f]
        rcv = kv_rcv.at[2 * kv_kind + f]
        if local:
            return pltpu.make_async_copy(tkv.at[f], dst, rcv)
        return remote(tkv.at[f], dst, kv_snd.at[2 * f + kk], rcv, dev(z, kk, kv_col))

    def finish(f, put):
        for j in range(4):
            i = chunk_of(f, j)
            total = own[i] + pin[i].astype(f32) + sin[i].astype(f32)
            put(j, (total * rinv[pl.ds(j, 1), :]).astype(bf16))

    def kv_prepare(g):
        for kind in range(2):
            pltpu.make_async_copy(tkv.at[0], kvt.at[kind, g], kv_rcv.at[2 * kind + g]).wait()
        picked = []
        for kind in range(2):
            acc = jnp.zeros((128, TOK), f32)
            for a in range(4):
                ohg = oh[pl.ds(pl.multiple_of(128 * xor2(c, a), 128), 128), :]
                acc = acc + jnp.dot(kvt[kind, g, a], ohg, preferred_element_type=f32)
            picked.append(acc)
        lo, hi = picked[0][:64], picked[0][64:]
        cos = jnp.concatenate([rope[2]] * 2, axis=1)
        sine = jnp.concatenate([rope[3]] * 2, axis=1)
        rot = jnp.concatenate([lo * cos - hi * sine, hi * cos + lo * sine], axis=0)
        keys[g] = rot.T.astype(bf16)
        vals[g] = picked[1].astype(bf16)

    def attend(f):
        g = lax.div(f, 4)
        table = jnp.concatenate(
            [jnp.concatenate([tq[f, kk, j] for j in range(4)], axis=1) for kk in range(2)], axis=0
        )
        picked = jnp.dot(table, oh[...], preferred_element_type=f32)
        cos = jnp.concatenate([rope[0]] * 2, axis=1)
        sine = jnp.concatenate([rope[1]] * 2, axis=1)
        q = []
        for kk in range(2):
            lo, hi = picked[128 * kk : 128 * kk + 64], picked[128 * kk + 64 : 128 * kk + 128]
            q.append(jnp.concatenate([lo * cos - hi * sine, hi * cos + lo * sine], axis=0).astype(bf16))
        blocks = [(s, b) for s in range(2) for b in range(2)]
        scores = []
        for s, b in blocks:
            at = SEQ * s + 128 * b
            both = jnp.concatenate([v[:, at : at + 128] for v in q], axis=1)
            rows = keys[g, pl.ds(SEQ * s, 128 * (b + 1)), :]
            scores.append(jnp.dot(rows, both, preferred_element_type=f32))
        sums = []
        for (s, b), sc in zip(blocks, scores):
            n = 128 * (b + 1)
            es, dens = [], []
            for kk in range(2):
                x = sc[:, 128 * kk : 128 * kk + 128] + bias[s, :n, 128 * b : 128 * b + 128]
                e = jnp.exp2(x - jnp.max(x, axis=0, keepdims=True))
                dens.append(jnp.sum(e, axis=0, keepdims=True))
                es.append(e.astype(bf16))
            o = jnp.dot(
                vals[g, :, pl.ds(SEQ * s, n)], jnp.concatenate(es, axis=1), preferred_element_type=f32
            )
            sums.append((o, dens))
        for (s, b), (o, dens) in zip(blocks, sums):
            for kk in range(2):
                part = o[:, 128 * kk : 128 * kk + 128] * (1.0 / dens[kk])
                at = pl.multiple_of(256 * f + 128 * kk, 128)
                out_ref[pl.ds(SEQ * s + 128 * b, 128), pl.ds(at, 128)] = part.T.astype(bf16)

    unit_wide(jnp.int32(0))

    def step(i, carry):
        even = lax.rem(i, 2) == 0
        u = lax.div(i, 2) + 1

        @pl.when(i == 4)
        def _():
            for n in (0, 1):
                hop_c(0, 1, n).wait_recv()
                hop_c(1, 2, n).start()

        for at, n in ((6, 3), (8, 2)):

            @pl.when(i == at)
            def _():
                hop_c(0, 2, n).wait_recv()
                hop_c(2, 1, n).start()

        @pl.when(i == 8)
        def _():
            for n in (3, 2):
                hop_c(0, 1, n).wait_recv()
            take(1)

        @pl.when(i == 14)
        def _():
            for n in (0, 1):
                hop_c(0, 2, n).wait_recv()
            take(2)
            for n in (0, 1):
                hop_c(1, 2, n).wait_recv()
            for n in (3, 2):
                hop_c(2, 1, n).wait_recv()
            take(3)

        @pl.when(i == 15)
        def _():
            for j in range(4):
                square(j)
            for n in range(1, 2 * NZ):
                ss_copy(n).start()

        deep = (u >= 8) & (u != 14) & (u != 17)

        @pl.when(even & (u < UNITS) & deep)
        def _():
            unit_deep(u)

        @pl.when(even & (u < UNITS) & jnp.logical_not(deep))
        def _():
            unit_wide(u)

        @pl.when(even & (u <= UNITS))
        def _():
            x_copy(u - 1).wait_recv()
            for h in range(2):
                own[2 * (u - 1) + h] = own[2 * (u - 1) + h] + xr[2 * (u - 1) + h].astype(f32)

        @pl.when(z < NZ // 2)
        def _():
            move_up(i - LAG * z - k)
            move_down(i - LAG * (NZ - 1 - z) - k)

        @pl.when(z >= NZ // 2)
        def _():
            move_down(i - LAG * (NZ - 1 - z) - k)
            move_up(i - LAG * z - k)

        last = i - LAG * (NZ - 1)

        @pl.when(last == 16)
        def _():
            total = ss_own[...]
            for n in range(1, 2 * NZ):
                ss_copy(n).wait_recv()
                total = total + ss_in[n - 1]
            rinv[...] = lax.rsqrt(total * (1.0 / 8192.0) + epsilon)

        @pl.when((last == 17) | (last == 19))
        def _():
            f = lax.div(last - 17, 2)

            def put(j, v):
                tkv[f, xor2(c, j)] = v

            finish(f, put)
            for kk in range(2):
                me = (kv_col == c) & (k == kk)

                @pl.when(me)
                def _():
                    kv_copy(f, kk, True).start()

                @pl.when(jnp.logical_not(me))
                def _():
                    kv_copy(f, kk, False).start()

        gap = (last == 29) | (last == 35)

        @pl.when((last >= 21) & (last < CHUNKS) & (lax.rem(last, 2) == 1) & jnp.logical_not(gap))
        def _():
            f = lax.div(last - jnp.where(last < 29, 21, jnp.where(last < 35, 23, 25)), 2)

            def put(j, v):
                tq[f, k, j] = v

            finish(f + 2, put)
            t_copy(f).start()

        @pl.when(last == 24)
        def _():
            kv_prepare(0)

        @pl.when(last == 30)
        def _():
            kv_prepare(1)

        w0 = last - 25
        f_now = lax.div(w0, 2) - jnp.where(last < 37, 0, 1)

        @pl.when((w0 >= 0) & (lax.rem(w0, 2) == 0) & (last != 37))
        def _():
            t_copy(f_now).wait_recv()
            attend(f_now)

        return carry

    lax.fori_loop(0, CHUNKS + LAG * (NZ - 1) + 2, step, 0)

    for j in range(4):
        for kk in range(2):
            if j or kk:
                hop_a(j, kk).wait_send()
        t = xor2(c, j)

        @pl.when(t != z)
        def _():
            for kk in range(2):
                src, dst = hop_b(t, z, kk)
                remote(src, dst, b_snd.at[2 * t + kk], b_rcv.at[2 * z + kk], dev(t, k, c)).wait_send()

    for n in range(NZ):
        hop_c(0, 1, n).wait_send()
        hop_c(0, 2, n).wait_send()
        if n < 2:
            hop_c(1, 2, n).wait_send()
        else:
            hop_c(2, 1, n).wait_send()

    def drain_units(u, carry):
        x_copy(u).wait_send()

        @pl.when(z < NZ - 1)
        def _():
            up_copy(u).wait_send()

        @pl.when(z > 0)
        def _():
            down_copy(u).wait_send()

        return carry

    lax.fori_loop(0, UNITS, drain_units, 0)
    for n in range(1, 2 * NZ):
        ss_copy(n).wait_send()
    for f in range(2):
        for kk in range(2):

            @pl.when(jnp.logical_not((kv_col == c) & (k == kk)))
            def _():
                kv_copy(f, kk, False).wait_send()

    def drain_heads(f, carry):
        t_copy(f).wait_send()
        return carry

    lax.fori_loop(0, 8, drain_heads, 0)


def square_form(token_ids, seq_lengths, embed_table, norm_gain, query_weight, kv_weight):
    bf16, f32 = jnp.bfloat16, jnp.float32
    vm = pltpu.VMEM
    dma = pltpu.SemaphoreType.DMA
    vspec = pl.BlockSpec(memory_space=pltpu.VMEM)
    aspec = pl.BlockSpec(memory_space=pltpu.HBM)
    return pl.pallas_call(
        fused,
        out_shape=pltpu.VMEM((TOK, 2048), bf16),
        in_specs=[aspec] * 7,
        out_specs=vspec,
        scratch_shapes=[
            vm((1, TOK), jnp.int32),
            pltpu.SMEM((2,), jnp.int32),
            vm((64, 2048), bf16),
            vm((1, KD), f32),
            vm((4, HD // 2, SEQ), f32),
            vm((2560, KD), bf16),
            vm((128, KD), bf16),
            vm((VROWS, KD), bf16),
            vm((VROWS, KD), bf16),
            vm((CHUNKS, 128, 128), f32),
            vm((CHUNKS, 128, 128), bf16),
            vm((CHUNKS, 128, 128), bf16),
            vm((CHUNKS, 128, 128), bf16),
            vm((CHUNKS, 128, 128), bf16),
            vm((CHUNKS, 128, 128), bf16),
            vm((CHUNKS, 128, 128), bf16),
            vm((2 * NZ - 1, 8, 128), f32),
            vm((8, 128), f32),
            vm((8, 128), f32),
            vm((2, 4, 128, 128), bf16),
            vm((2, 2, 4, 128, 128), bf16),
            vm((8, 2, 4, 128, 128), bf16),
            vm((VROWS, TOK), bf16),
            vm((2, SEQ, SEQ), f32),
            vm((2, TOK, 128), bf16),
            vm((2, 128, TOK), bf16),
            dma((5,)),
            dma((20,)),
            dma((8,)), dma((8,)),
            dma((2 * NZ,)), dma((2 * NZ,)),
            dma((12,)), dma((12,)),
            dma((UNITS,)), dma((UNITS,)),
            dma((UNITS,)), dma((UNITS,)),
            dma((UNITS,)), dma((UNITS,)),
            dma((2 * NZ - 1,)), dma((2 * NZ - 1,)),
            dma((4,)), dma((4,)),
            dma((8,)), dma((8,)),
        ],
        cost_estimate=pl.CostEstimate(flops=6 * 10**9, bytes_accessed=8 * 10**6, transcendentals=2 * 10**6),
        compiler_params=pltpu.CompilerParams(
            collective_id=0, has_side_effects=True, vmem_limit_bytes=60 * 1024 * 1024
        ),
        name="fused",
    )(
        token_ids.reshape(1, TOK),
        seq_lengths,
        embed_table,
        norm_gain.reshape(1, -1),
        jnp.asarray(rope_constants()),
        query_weight,
        kv_weight,
    )


def solution(mesh):
    dp, tensor = mesh.shape["dp"], mesh.shape["tensor"]
    placed = (P("dp"), P("dp"), P("dp", "tensor"), P(), P("tensor", "dp"), P("tensor", "dp"))

    def on_device(*args):
        tokens, lengths, table, gain, qw, kvw = args
        square = (
            (dp, tensor) == (2 * NZ, 4)
            and tokens.shape == (TOK,)
            and lengths.shape == (2,)
            and table.shape == (64, 2048)
            and qw.shape == (2048, KD)
            and kvw.shape == (512, KD)
        )
        return square_form(*args) if square else general_form(*args)

    return jax.shard_map(
        on_device, mesh=mesh, in_specs=placed, out_specs=P("dp", "tensor"), check_vma=False
    )
```
